256 devices in a mesh: dom: 64 (over y, z, core), sub: 4 (over x).
Axes of the slice: x: 4, y: 4, z: 8, core: 2. Of those that a mesh axis runs over, the one named last changes fastest.
Arguments:
- displacement: float32 [3, 1048576], P(None, 'dom'), may hold values from -6 to 6
- connect: int32 [20, 196608], P(None, ('dom', 'sub')), may hold values from 0 to 20479
- shear: float32 [196608], P(('dom', 'sub')), may hold values from 0.3 to 3
- bulk: float32 [196608], P(('dom', 'sub')), may hold values from 0.3 to 3
- stiff_shear: float32 [60, 60], replicated, may hold values from -0.75 to 0.75
- stiff_bulk: float32 [60, 60], replicated, may hold values from -0.75 to 0.75
- seg_slave: int32 [8, 65536], P(None, ('dom', 'sub')), may hold values from 0 to 16383
- seg_part: int32 [65536, 1], P(('dom', 'sub')), may hold values from 0 to 63; in each aligned block of 256 rows (0 to 255, 256 to 511, ...) at most 8 rows name the same one
- seg_face: int32 [65536], P(('dom', 'sub')), may hold values from 0 to 2047
- face_nodes: int32 [8, 131072], P(None, 'dom'), may hold values from 0 to 16383
- dual: float32 [8, 65536], P(None, ('dom', 'sub')), may hold values from 0.2 to 2
- mortar: float32 [64, 65536], P(None, ('dom', 'sub')), may hold values from -4 to 4
- seg_count: int32 [256], P(('dom', 'sub')), may hold values from 128 to 256
Outputs:
- product: float32 [3, 1048576], P(None, ('dom', 'sub'))
The draws below stay inside these ranges and needn't reach their ends.
Inputs may be any that keep to these rules, and one draw needn't show every extreme that they name: `seg_part`: among the 256 segment slots of one device (live or not) no partition is named more than 8 times, a bound that some block reaches.
All inputs are finite; a program needn't handle non-finite values.
Results may differ from the reference program's by a relative error of at most 0.000067.
Values sent between devices are 32-bit elements; how exact they have to be, the bound alone decides.
No kernel may reach another device: no remote copies, remote signals or barrier semaphores. Data moves between devices by JAX's collectives and lax.ppermute only.
A program may use at most 128 MiB of HBM per device.

```python
import math
import jax
import jax.numpy as jnp
import numpy as np
from jax import lax

NODE = 16384
GHOST = 2048
ELEM = 768
SEG_DEV = 256
FACES = 2048
NODES = 1048576
ELEMS = 196608
SEGS = 65536
CAP = 8
FACES_ALL = 131072
N_DOM = 64
N_SUB = 4
DEVICES = 256


def plant(values, key, smallest, high):
    spot = [jax.random.randint(jax.random.fold_in(key, axis), (), 0, length) for axis, length in enumerate(values.shape)]
    main_axis = values.shape.index(max(values.shape))
    beside = spot[:main_axis] + [(spot[main_axis] + 1) % values.shape[main_axis]] + spot[main_axis + 1:]
    return values.at[tuple(spot)].set(smallest).at[tuple(beside)].set(high)


def block_levels(own_key, shape, split, smallest, high):
    def one(position, blocks):
        heights = jax.random.uniform(jax.random.fold_in(jax.random.fold_in(own_key, 6), position), (blocks,), jnp.float32, smallest / len(split), high / len(split))
        return jnp.repeat(jnp.exp(heights), shape[position] // blocks).reshape((-1,) + (1,) * (len(shape) - position - 1))

    factor_of = one(*split[0])
    for cut in split[1:]:
        factor_of = factor_of * one(*cut)
    return factor_of


def shared_out(stream_key, own, number, rows, amount, top, bound, lean):
    order = jax.random.permutation(stream_key, amount)
    crowded, common = portions_of(amount, rows * top, bound, lean, True), portions_of(amount, rows * top, bound, lean, False)
    places = jnp.arange(amount)

    def named(lengths, turn):
        used = int((lengths > 0).sum())
        fixed = max(1, used // 4)
        moved = fixed + (places - fixed + turn * (used - fixed)) % max(1, amount - fixed)
        return jnp.zeros((amount,), jnp.int32).at[order[jnp.where(places < fixed, places, moved)]].set(jnp.asarray(lengths, jnp.int32))

    lengths = jnp.where(number % 4 == 0, named(crowded, number // 4), named(common, number - number // 4 - 1))
    mixed = jax.random.permutation(jax.random.fold_in(own, 3), amount)
    donor, sink = mixed[0:amount // 2 * 2:2], mixed[1:amount // 2 * 2:2]
    slack = jnp.minimum(lengths[donor] - 1, bound - lengths[sink]) // 2
    slack = jnp.where((donor == order[0]) | (sink == order[0]) | (lengths[sink] == 0), 0, jnp.maximum(slack, 0))
    moved = jax.random.randint(jax.random.fold_in(own, 4), (amount // 2,), 0, 1 << 20) % (slack + 1)
    lengths = lengths.at[donor].add(-moved).at[sink].add(moved)
    labels = jnp.searchsorted(jnp.cumsum(lengths), jnp.arange(rows * top), side="right").astype(jnp.int32)
    listing = labels.reshape(top, rows).T
    listing = listing[jax.random.permutation(jax.random.fold_in(own, 1), rows)]
    turn = jax.random.randint(jax.random.fold_in(own, 2), (rows, 1), 0, top)
    return jnp.take_along_axis(listing, (jnp.arange(top)[None, :] + turn) % top, axis=1)


def portions_of(amount, total, bound, slope, full):
    portions = [(1 << 20) // math.isqrt(grade ** slope) + 1 for grade in range(1, amount + 1)]
    largest = bound if full else min(bound, max(-(-total // amount), total * portions[0] // sum(portions)))
    least = 1 if total - largest >= amount - 1 else 0
    given, spare = [largest] + [least] * (amount - 1), total - largest - least * (amount - 1)
    while spare > 0:
        free = [i for i in range(1, amount) if given[i] < largest] or [i for i in range(1, amount) if given[i] < bound]
        whole, remaining = sum([portions[i] for i in free]), spare
        for i in free:
            more = min(bound - given[i], max(1, remaining * portions[i] // whole), spare)
            given[i] = given[i] + more
            spare = spare - more
    return np.array(given)


def centred(stream_key, shape, scale, most, pieces=(), kind=jnp.bfloat16):
    array = jax.random.normal(stream_key, shape, jnp.float32) * scale
    if len(pieces) > 0:
        array = block_levels(stream_key, shape, pieces, -0.22, 0.18) * array
    return jnp.clip(array, min=-most, max=most).astype(kind)


def setup_inputs(seed: int = 0) -> dict:
    key_list = jax.random.split(jax.random.key(seed), 14)
    displacement = centred(key_list[0], (3, NODES), 1.0, 6.0, ((1, 64),), jnp.float32)
    connect = plant(jax.random.randint(key_list[1], (20, ELEMS), 0, NODE + 2 * GHOST), jax.random.fold_in(key_list[1], 1), 0, (NODE + 2 * GHOST) - 1).astype(jnp.int32)
    shear = jnp.clip(jnp.exp(math.log(3.0) - 2.3025851 * jax.random.uniform(key_list[2], (ELEMS,), jnp.float32) ** block_levels(key_list[2], (ELEMS,), ((0, 256),), -0.2, 0.2)), 0.3, 3.0)
    bulk = jnp.clip(jnp.exp(math.log(3.0) - 2.3025851 * jax.random.uniform(key_list[3], (ELEMS,), jnp.float32) ** block_levels(key_list[3], (ELEMS,), ((0, 256),), -0.2, 0.2)), 0.3, 3.0)
    stiff_shear = centred(key_list[4], (60, 60), 60 ** -0.5, 0.75, (), jnp.float32)
    stiff_bulk = centred(key_list[5], (60, 60), 60 ** -0.5, 0.75, (), jnp.float32)
    seg_slave = plant(jax.random.randint(key_list[6], (8, SEGS), 0, NODE), jax.random.fold_in(key_list[6], 1), 0, NODE - 1).astype(jnp.int32)
    seg_part_keys = jax.random.split(jax.random.fold_in(key_list[7], 1), SEGS // SEG_DEV)
    seg_part_turns = jax.random.permutation(jax.random.fold_in(key_list[7], 3), SEGS // SEG_DEV)
    seg_part = jax.vmap(lambda own, number: shared_out(jax.random.fold_in(key_list[7], 2), own, number, SEG_DEV, N_DOM, 1, CAP, 2))(seg_part_keys, seg_part_turns).reshape((SEGS, 1))
    seg_face = plant(jax.random.randint(key_list[8], (SEGS,), 0, FACES), jax.random.fold_in(key_list[8], 1), 0, FACES - 1).astype(jnp.int32)
    face_nodes = plant(jax.random.randint(key_list[9], (8, FACES_ALL), 0, NODE), jax.random.fold_in(key_list[9], 1), 0, NODE - 1).astype(jnp.int32)
    dual = jnp.clip(jnp.exp(math.log(2.0) - 2.3025851 * jax.random.uniform(key_list[10], (8, SEGS), jnp.float32) ** block_levels(key_list[10], (8, SEGS), ((1, 256),), -0.2, 0.2)), 0.2, 2.0)
    mortar = centred(key_list[11], (64, SEGS), 0.3, 4.0, ((1, 256),), jnp.float32)
    seg_count = plant(jax.random.randint(key_list[12], (DEVICES,), SEG_DEV // 2, SEG_DEV + 1), jax.random.fold_in(key_list[12], 1), SEG_DEV // 2, SEG_DEV).astype(jnp.int32)
    return {"displacement": displacement, "connect": connect, "shear": shear, "bulk": bulk, "stiff_shear": stiff_shear, "stiff_bulk": stiff_bulk, "seg_slave": seg_slave, "seg_part": seg_part, "seg_face": seg_face, "face_nodes": face_nodes, "dual": dual, "mortar": mortar, "seg_count": seg_count}


penalty = 2.0


def reference(displacement, connect, shear, bulk, stiff_shear, stiff_bulk, seg_slave, seg_part, seg_face, face_nodes, dual, mortar, seg_count):
    highest = lax.Precision.HIGHEST
    total = NODE * N_DOM
    owner = jnp.arange(ELEMS, dtype=jnp.int32) // (ELEM * N_SUB)
    global_ids = owner[None, :] * NODE + connect - GHOST
    inside = ((global_ids >= 0) & (global_ids < total)).astype(jnp.float32)
    safe_ids = jnp.clip(global_ids, 0, total - 1).astype(jnp.int32)
    gathered = (displacement[:, safe_ids] * inside[None]).reshape(60, ELEMS)
    forces = shear * jnp.dot(stiff_shear.T, gathered, precision=highest) + bulk * jnp.dot(stiff_bulk.T, gathered, precision=highest)
    result = jnp.zeros((3, total), jnp.float32).at[:, safe_ids].add(forces.reshape(3, 20, ELEMS) * inside[None])
    seg_ids = jnp.arange(SEGS, dtype=jnp.int32)
    slave_owner = seg_ids // (SEG_DEV * N_SUB)
    slave_ids = (slave_owner[None, :] * NODE + seg_slave).astype(jnp.int32)
    target = seg_part[:, 0]
    master_local = face_nodes[:, (target * FACES + seg_face).astype(jnp.int32)]
    master_ids = (target[None, :] * NODE + master_local).astype(jnp.int32)
    live = ((seg_ids % SEG_DEV) < seg_count[seg_ids // SEG_DEV]).astype(jnp.float32)
    matrix = mortar.reshape(8, 8, SEGS)
    slave_vals = displacement[:, slave_ids]
    master_vals = displacement[:, master_ids]
    gap = dual[None] * slave_vals - jnp.einsum("ijs,cjs->cis", matrix, master_vals, precision=highest)
    mult = penalty * gap * live[None, None]
    result = result.at[:, slave_ids].add(dual[None] * mult)
    result = result.at[:, master_ids].add(-jnp.einsum("ijs,cis->cjs", matrix, mult, precision=highest))
    return result
```

```python
import jax
import jax.numpy as jnp
from jax import lax
from jax.experimental import pallas as pl
from jax.experimental.pallas import tpu as pltpu
from jax.sharding import PartitionSpec as P

GHOST = 2048
LO = 256
penalty = 2.0
F32 = jnp.float32
BF16 = jnp.bfloat16


def pieces(x):
    first = x.astype(BF16)
    second = (x - first.astype(F32)).astype(BF16)
    return first, second


def one_hot_lo(index):
    n = index.shape[1]
    rows = lax.broadcasted_iota(jnp.int32, (LO, n), 0)
    return jnp.where(rows == (index & (LO - 1)), 1.0, 0.0).astype(BF16)


def hi_mask(index, rows):
    n = index.shape[1]
    return lax.broadcasted_iota(jnp.int32, (rows, n), 0) == (index >> 8)


def to_rows(source, offset, count, target, first_row, stride):
    for c in range(3):
        for h in range(count):
            row = c * stride + first_row + h
            target[row : row + 1, :] = source[c : c + 1, offset + h * LO : offset + (h + 1) * LO]


def gather_column(table, index, rows):
    hot = one_hot_lo(index)
    picked = jnp.dot(table, jnp.concatenate([hot, hot], axis=0), preferred_element_type=F32)
    mask = hi_mask(index, rows)
    return [
        jnp.sum(jnp.where(mask, picked[c * rows : (c + 1) * rows], 0.0), axis=0, keepdims=True)
        for c in range(3)
    ]


def scatter_column(values, index, rows):
    hot = one_hot_lo(index)
    mask = hi_mask(index, rows)
    firsts, seconds = [], []
    for c in range(3):
        first, second = pieces(values[c])
        firsts.append(jnp.where(mask, first.astype(F32), 0.0).astype(BF16))
        seconds.append(jnp.where(mask, second.astype(F32), 0.0).astype(BF16))
    spread = jnp.concatenate(
        [jnp.concatenate(firsts, axis=0), jnp.concatenate(seconds, axis=0)], axis=1
    )
    return lax.dot_general(
        spread,
        jnp.concatenate([hot, hot], axis=1),
        (((1,), (1,)), ((), ())),
        preferred_element_type=F32,
    )


def forces_kernel(disp, before, after, connect, shear, bulk, k_shear, k_bulk, out, rows, table, dofs):
    nodes = disp.shape[1]
    ghost = GHOST // LO
    total = nodes // LO + 2 * ghost
    to_rows(before, 0, ghost, rows, 0, total)
    to_rows(disp, 0, nodes // LO, rows, ghost, total)
    to_rows(after, 0, ghost, rows, total - ghost, total)
    first, second = pieces(rows[...])
    table[:, :LO] = first
    table[:, LO:] = second
    dofs[...] = jnp.zeros_like(dofs)

    def step(a, carry):
        got = gather_column(table[...], connect[pl.ds(a, 1), :], total)
        for c in range(3):
            dofs[pl.ds(20 * c + a, 1), :] = got[c]
        return carry

    lax.fori_loop(0, 20, step, 0)
    g_first, g_second = pieces(dofs[...])
    g = jnp.concatenate([g_first, g_first, g_second, g_second], axis=0)

    def product(k):
        k_first, k_second = pieces(k[...])
        wide = jnp.concatenate([k_first, k_second, k_first, k_second], axis=1)
        return jnp.dot(wide, g, preferred_element_type=F32)

    out[...] = shear[...] * product(k_shear) + bulk[...] * product(k_bulk)


def element_scatter_kernel(forces, connect, owned, low, high, total):
    ghost = GHOST // LO
    all_rows = total.shape[0] // 3
    total[...] = jnp.zeros_like(total)

    def step(a, carry):
        values = [forces[pl.ds(20 * c + a, 1), :] for c in range(3)]
        total[...] += scatter_column(values, connect[pl.ds(a, 1), :], all_rows)
        return carry

    lax.fori_loop(0, 20, step, 0)
    own = all_rows - 2 * ghost
    for c in range(3):
        base = c * all_rows
        low[c * ghost : (c + 1) * ghost, :] = total[base : base + ghost, :]
        owned[c * own : (c + 1) * own, :] = total[base + ghost : base + ghost + own, :]
        high[c * ghost : (c + 1) * ghost, :] = total[base + ghost + own : base + all_rows, :]


def pack_kernel(disp, slave, dual, mortar, face, part, count, out, slot_out, rows, table):
    segs = slave.shape[1]
    own = disp.shape[1] // LO
    to_rows(disp, 0, own, rows, 0, own)
    first, second = pieces(rows[...])
    packed = jnp.concatenate([first, second], axis=1)
    cap = 8
    width = out.shape[0]
    n_dom = width // cap
    lanes = lax.broadcasted_iota(jnp.int32, (1, segs), 1)
    live = jnp.where(lanes < count[0, 0], 1.0, 0.0)
    vals = []
    for i in range(8):
        vals.append(gather_column(packed, slave[i : i + 1, :], own))
    slave_part = [
        (dual[i : i + 1, :] * live) * vals[i][c] for c in range(3) for i in range(8)
    ]
    payload = jnp.concatenate(
        slave_part
        + [mortar[...] * live, face[...].astype(F32), jnp.zeros((39, segs), F32)],
        axis=0,
    )
    hits = lax.broadcasted_iota(jnp.int32, (n_dom, segs), 0) == part[...]
    hits_b = jnp.where(hits, 1.0, 0.0).astype(BF16)
    earlier = (
        lax.broadcasted_iota(jnp.int32, (segs, segs), 0)
        < lax.broadcasted_iota(jnp.int32, (segs, segs), 1)
    )
    before = jnp.dot(
        hits_b, jnp.where(earlier, 1.0, 0.0).astype(BF16), preferred_element_type=F32
    )
    rank = jnp.sum(jnp.where(hits, before, 0.0), axis=0, keepdims=True).astype(jnp.int32)
    slot = part[...] * cap + rank
    slot_out[...] = slot
    place = jnp.where(
        lax.broadcasted_iota(jnp.int32, (width, segs), 0) == slot, 1.0, 0.0
    ).astype(BF16)
    p1 = payload.astype(BF16)
    rest = payload - p1.astype(F32)
    p2 = rest.astype(BF16)
    p3 = (rest - p2.astype(F32)).astype(BF16)
    out[...] = lax.dot_general(
        jnp.concatenate([place, place, place], axis=1),
        jnp.concatenate([p1, p2, p3], axis=1),
        (((1,), (1,)), ((), ())),
        preferred_element_type=F32,
    )


def master_kernel(incoming, disp, faces, mult_out, force_out, nodes_out, rows):
    own = disp.shape[1] // LO
    width = incoming.shape[0]
    n_dom = width // 8
    to_rows(disp, 0, own, rows, 0, own)
    first, second = pieces(rows[...])
    packed = jnp.concatenate([first, second], axis=1)
    got = incoming[...].T
    face = got[88:89, :].astype(jnp.int32)
    groups = faces.shape[1] // LO
    listing = jnp.concatenate([faces[:, g * LO : (g + 1) * LO] for g in range(groups)], axis=0)
    f_first = (listing >> 7).astype(F32).astype(BF16)
    f_second = (listing & 127).astype(F32).astype(BF16)
    hot = one_hot_lo(face)
    f_table = jnp.concatenate([f_first, f_second], axis=0)
    picked = jnp.dot(f_table, hot, preferred_element_type=F32)
    both = picked[: 8 * groups] * 128.0 + picked[8 * groups :]
    face_hi = face >> 8
    nodes = jnp.zeros((8, width), F32)
    for g in range(groups):
        nodes = nodes + jnp.where(face_hi == g, both[8 * g : 8 * (g + 1)], 0.0)
    nodes = nodes.astype(jnp.int32)
    nodes_out[...] = nodes
    vals = [gather_column(packed, nodes[j : j + 1, :], own) for j in range(8)]
    matrix = [got[24 + 8 * i : 32 + 8 * i, :] for i in range(8)]
    mults = []
    for c in range(3):
        master = jnp.concatenate([vals[j][c] for j in range(8)], axis=0)
        force = jnp.zeros((8, width), F32)
        for i in range(8):
            gap = got[8 * c + i : 8 * c + i + 1, :] - jnp.sum(
                matrix[i] * master, axis=0, keepdims=True
            )
            mult = penalty * gap
            mults.append(mult)
            force = force - matrix[i] * mult
        force_out[8 * c : 8 * c + 8, :] = force
    back = jnp.concatenate(mults + [jnp.zeros((8, width), F32)], axis=0).T
    back = back.reshape(n_dom, 8, 32)
    for k in range(8):
        mult_out[:, 0, 32 * k : 32 * (k + 1)] = back[:, k, :]


def master_scatter_kernel(force, nodes, out):
    own = out.shape[0] // 3
    total = jnp.zeros(out.shape, F32)
    for j in range(8):
        values = [force[8 * c + j : 8 * c + j + 1, :] for c in range(3)]
        total = total + scatter_column(values, nodes[j : j + 1, :], own)
    out[...] = total


def slave_kernel(returned, slot, dual, slave, owned, master, upper, lower, out):
    own = owned.shape[0] // 3
    ghost = upper.shape[0] // 3
    segs = slot.shape[1]
    n_dom = returned.shape[0]
    mult_rows = returned[...].reshape(n_dom, 256).T
    m1 = mult_rows.astype(BF16)
    rest = mult_rows - m1.astype(F32)
    m2 = rest.astype(BF16)
    m3 = (rest - m2.astype(F32)).astype(BF16)
    hot = jnp.where(
        lax.broadcasted_iota(jnp.int32, (n_dom, segs), 0) == (slot[...] >> 3), 1.0, 0.0
    ).astype(BF16)
    picked = jnp.dot(
        jnp.concatenate([m1, m2, m3], axis=1),
        jnp.concatenate([hot, hot, hot], axis=0),
        preferred_element_type=F32,
    )
    rank = slot[...] & 7
    mult = jnp.zeros((32, segs), F32)
    for k in range(8):
        mult = mult + jnp.where(rank == k, picked[32 * k : 32 * (k + 1)], 0.0)
    total = owned[...] + master[...]
    for i in range(8):
        values = [dual[i : i + 1, :] * mult[8 * c + i : 8 * c + i + 1, :] for c in range(3)]
        total = total + scatter_column(values, slave[i : i + 1, :], own)
    quarters = out.shape[0]
    per = own // quarters
    for c in range(3):
        block = total[c * own : (c + 1) * own]
        for q in range(quarters):
            part = block[q * per : (q + 1) * per]
            if q == 0:
                part = jnp.concatenate(
                    [part[:ghost] + lower[c * ghost : (c + 1) * ghost, :], part[ghost:]], axis=0
                )
            if q == quarters - 1:
                part = jnp.concatenate(
                    [part[:-ghost], part[-ghost:] + upper[c * ghost : (c + 1) * ghost, :]], axis=0
                )
            out[q, c * per : (c + 1) * per, :] = part


def finish_kernel(own_part, a, b, d, out):
    per = own_part.shape[0] // 3
    total = own_part[...] + a[...] + b[...] + d[...]
    for c in range(3):
        for h in range(per):
            out[c : c + 1, h * LO : (h + 1) * LO] = total[c * per + h : c * per + h + 1, :]


def call(kernel, outs, *args, scratch=(), smem=()):
    specs = [
        pl.BlockSpec(memory_space=pltpu.SMEM if i in smem else pltpu.VMEM)
        for i in range(len(args))
    ]
    many = isinstance(outs, list)
    return pl.pallas_call(
        kernel,
        out_shape=outs,
        in_specs=specs,
        out_specs=[pl.BlockSpec(memory_space=pltpu.VMEM)] * len(outs)
        if many
        else pl.BlockSpec(memory_space=pltpu.VMEM),
        scratch_shapes=list(scratch),
        compiler_params=pltpu.CompilerParams(vmem_limit_bytes=48 * 1024 * 1024),
    )(*args)


def shape(*dims):
    return jax.ShapeDtypeStruct(dims, F32)


def element_forces(displacement, before, after, connect, shear, bulk, k_shear, k_bulk):
    nodes = displacement.shape[1]
    rows = nodes // LO + 2 * GHOST // LO
    elems = connect.shape[1]
    k_shear = jnp.pad(k_shear.T, ((0, 4), (0, 4)))
    k_bulk = jnp.pad(k_bulk.T, ((0, 4), (0, 4)))
    return call(
        forces_kernel,
        shape(64, elems),
        displacement,
        before,
        after,
        connect,
        shear[None],
        bulk[None],
        k_shear,
        k_bulk,
        scratch=[
            pltpu.VMEM((3 * rows, LO), F32),
            pltpu.VMEM((3 * rows, 2 * LO), BF16),
            pltpu.VMEM((64, elems), F32),
        ],
    )


def element_scatter(forces, connect, nodes):
    own = nodes // LO
    ghost = GHOST // LO
    return call(
        element_scatter_kernel,
        [shape(3 * own, LO), shape(3 * ghost, LO), shape(3 * ghost, LO)],
        forces,
        connect,
        scratch=[pltpu.VMEM((3 * (own + 2 * ghost), LO), F32)],
    )


def pack(displacement, seg_slave, dual, mortar, seg_face, seg_part, seg_count, n_dom):
    own = displacement.shape[1] // LO
    segs = seg_face.shape[0]
    return call(
        pack_kernel,
        [shape(n_dom * 8, 128), jax.ShapeDtypeStruct((1, segs), jnp.int32)],
        displacement,
        seg_slave,
        dual,
        mortar,
        seg_face[None],
        seg_part.reshape(1, segs),
        seg_count.reshape(1, 1),
        smem=(6,),
        scratch=[pltpu.VMEM((3 * own, LO), F32), pltpu.VMEM((3 * own, 2 * LO), BF16)],
    )


def master(incoming, displacement, face_nodes):
    own = displacement.shape[1] // LO
    width = incoming.shape[0]
    return call(
        master_kernel,
        [
            shape(width // 8, 1, 256),
            shape(24, width),
            jax.ShapeDtypeStruct((8, width), jnp.int32),
        ],
        incoming,
        displacement,
        face_nodes,
        scratch=[pltpu.VMEM((3 * own, LO), F32)],
    )


def slave_side(returned, slot, dual, seg_slave, owned, master_part, upper, lower, n_sub):
    own = owned.shape[0] // 3
    return call(
        slave_kernel,
        shape(n_sub, 3 * own // n_sub, LO),
        returned,
        slot,
        dual,
        seg_slave,
        owned,
        master_part,
        upper,
        lower,
    )


def on_device(
    displacement,
    connect,
    shear,
    bulk,
    stiff_shear,
    stiff_bulk,
    seg_slave,
    seg_part,
    seg_face,
    face_nodes,
    dual,
    mortar,
    seg_count,
):
    nodes = displacement.shape[1]
    n_dom, n_sub = lax.axis_size("dom"), lax.axis_size("sub")
    up = [(i, i + 1) for i in range(n_dom - 1)]
    down = [(i + 1, i) for i in range(n_dom - 1)]
    before = lax.ppermute(displacement[:, nodes - GHOST :], "dom", up)
    after = lax.ppermute(displacement[:, :GHOST], "dom", down)
    outgoing, slot = pack(
        displacement, seg_slave, dual, mortar, seg_face, seg_part, seg_count, n_dom
    )
    incoming = lax.all_to_all(
        outgoing.reshape(n_dom, 8, 128), "dom", split_axis=0, concat_axis=0, tiled=True
    )
    forces = element_forces(
        displacement, before, after, connect, shear, bulk, stiff_shear, stiff_bulk
    )
    mult, master_force, master_nodes = master(
        incoming.reshape(n_dom * 8, 128), displacement, face_nodes
    )
    returned = lax.all_to_all(mult, "dom", split_axis=0, concat_axis=0, tiled=True)
    owned, low, high = element_scatter(forces, connect, nodes)
    upper = lax.ppermute(low, "dom", down)
    lower = lax.ppermute(high, "dom", up)
    master_part = call(
        master_scatter_kernel, shape(3 * nodes // LO, LO), master_force, master_nodes
    )
    blocks = slave_side(
        returned, slot, dual, seg_slave, owned, master_part, upper, lower, n_sub
    )
    me = lax.axis_index("sub")
    sent = [
        lax.ppermute(
            lax.dynamic_index_in_dim(blocks, (me + k) % n_sub, 0, keepdims=False),
            "sub",
            [(s, (s + k) % n_sub) for s in range(n_sub)],
        )
        for k in range(1, n_sub)
    ]
    mine = lax.dynamic_index_in_dim(blocks, me, 0, keepdims=False)
    return call(finish_kernel, shape(3, nodes // n_sub), mine, *sent)


def solution(mesh):
    placed = (
        P(None, "dom"),
        P(None, ("dom", "sub")),
        P(("dom", "sub")),
        P(("dom", "sub")),
        P(),
        P(),
        P(None, ("dom", "sub")),
        P(("dom", "sub"), None),
        P(("dom", "sub")),
        P(None, "dom"),
        P(None, ("dom", "sub")),
        P(None, ("dom", "sub")),
        P(("dom", "sub")),
    )
    return jax.shard_map(
        on_device, mesh=mesh, in_specs=placed, out_specs=P(None, ("dom", "sub")), check_vma=False
    )
```

```python
import jax
import jax.numpy as jnp
from jax import lax
from jax.experimental import pallas as pl
from jax.experimental.pallas import tpu as pltpu
from jax.sharding import PartitionSpec as P

GHOST = 2048
LO = 256
penalty = 2.0
F32 = jnp.float32
BF16 = jnp.bfloat16


def pieces(x):
    first = x.astype(BF16)
    second = (x - first.astype(F32)).astype(BF16)
    return first, second


def one_hot_lo(index):
    n = index.shape[1]
    rows = lax.broadcasted_iota(jnp.int16, (LO, n), 0)
    low = (index & (LO - 1)).astype(jnp.int16)
    return jnp.where(rows == low, jnp.bfloat16(1), jnp.bfloat16(0))


def hi_mask(index, rows):
    n = index.shape[1]
    return lax.broadcasted_iota(jnp.int32, (rows, n), 0) == (index >> 8)


def to_rows(source, offset, count, target, first_row, stride):
    for c in range(3):
        for h in range(count):
            row = c * stride + first_row + h
            target[row : row + 1, :] = source[c : c + 1, offset + h * LO : offset + (h + 1) * LO]


def gather_column(table, index, rows):
    hot = one_hot_lo(index)
    picked = jnp.dot(table, jnp.concatenate([hot, hot], axis=0), preferred_element_type=F32)
    mask = hi_mask(index, rows)
    return [
        jnp.sum(jnp.where(mask, picked[c * rows : (c + 1) * rows], 0.0), axis=0, keepdims=True)
        for c in range(3)
    ]


def scatter_column(values, index, rows):
    hot = one_hot_lo(index)
    mask = hi_mask(index, rows)
    firsts, seconds = [], []
    for c in range(3):
        first, second = pieces(values[c])
        firsts.append(jnp.where(mask, first.astype(F32), 0.0).astype(BF16))
        seconds.append(jnp.where(mask, second.astype(F32), 0.0).astype(BF16))
    spread = jnp.concatenate(
        [jnp.concatenate(firsts, axis=0), jnp.concatenate(seconds, axis=0)], axis=1
    )
    return lax.dot_general(
        spread,
        jnp.concatenate([hot, hot], axis=1),
        (((1,), (1,)), ((), ())),
        preferred_element_type=F32,
    )


def forces_kernel(own, before, after, connect, shear, bulk, k_shear, k_bulk, out, table, dofs, k_pad):
    ghost = before.shape[0] // 3
    count = own.shape[0] // 3
    total = count + 2 * ghost
    for source, first_row, rows in ((before, 0, ghost), (after, total - ghost, ghost)):
        first, second = pieces(source[...])
        for c in range(3):
            here = slice(c * total + first_row, c * total + first_row + rows)
            table[here, :LO] = first[c * rows : (c + 1) * rows]
            table[here, LO:] = second[c * rows : (c + 1) * rows]
    for c in range(3):
        table[c * total + ghost : c * total + ghost + count, :] = own[c * count : (c + 1) * count, :]
    dofs[...] = jnp.zeros_like(dofs)

    def step(a, carry):
        got = gather_column(table[...], connect[pl.ds(a, 1), :], total)
        for c in range(3):
            dofs[pl.ds(20 * c + a, 1), :] = got[c]
        return carry

    lax.fori_loop(0, 20, step, 0, unroll=True)
    g_first, g_second = pieces(dofs[...])
    g = jnp.concatenate([g_first, g_first, g_second, g_second], axis=0)

    def product(k):
        k_pad[...] = jnp.zeros_like(k_pad)
        k_pad[: k.shape[0], : k.shape[1]] = k[...]
        k_first, k_second = pieces(k_pad[...].T)
        wide = jnp.concatenate([k_first, k_second, k_first, k_second], axis=1)
        return jnp.dot(wide, g, preferred_element_type=F32)

    out[...] = shear[...] * product(k_shear) + bulk[...] * product(k_bulk)


def element_scatter_kernel(forces, connect, owned, low, high, total):
    ghost = GHOST // LO
    all_rows = total.shape[0] // 3
    total[...] = jnp.zeros_like(total)

    def step(a, carry):
        values = [forces[pl.ds(20 * c + a, 1), :] for c in range(3)]
        total[...] += scatter_column(values, connect[pl.ds(a, 1), :], all_rows)
        return carry

    lax.fori_loop(0, 20, step, 0, unroll=True)
    own = all_rows - 2 * ghost
    for c in range(3):
        base = c * all_rows
        low[c * ghost : (c + 1) * ghost, :] = total[base : base + ghost, :]
        owned[c * own : (c + 1) * own, :] = total[base + ghost : base + ghost + own, :]
        high[c * ghost : (c + 1) * ghost, :] = total[base + ghost + own : base + all_rows, :]


def pack_kernel(*refs):
    given, (count, out, slot_out, table, head, tail, rows) = refs[:6], refs[6:13]
    held, sems = refs[13:19], refs[19]
    copies = [pltpu.make_async_copy(a, b, sems.at[i]) for i, (a, b) in enumerate(zip(given, held))]
    for copy in copies:
        copy.start()
    for copy in copies:
        copy.wait()
    disp, slave, dual, mortar, face, part = held
    segs = slave.shape[1]
    own = disp.shape[1] // LO
    to_rows(disp, 0, own, rows, 0, own)
    first, second = pieces(rows[...])
    packed = jnp.concatenate([first, second], axis=1)
    table[...] = packed
    ghost = GHOST // LO
    for c in range(3):
        head[c * ghost : (c + 1) * ghost, :] = rows[c * own : c * own + ghost, :]
        tail[c * ghost : (c + 1) * ghost, :] = rows[(c + 1) * own - ghost : (c + 1) * own, :]
    cap = 8
    width = out.shape[0]
    n_dom = width // cap
    lanes = lax.broadcasted_iota(jnp.int32, (1, segs), 1)
    live = jnp.where(lanes < count[0, 0], 1.0, 0.0)
    vals = []
    for i in range(8):
        vals.append(gather_column(packed, slave[i : i + 1, :], own))
    slave_part = [
        (dual[i : i + 1, :] * live) * vals[i][c] for c in range(3) for i in range(8)
    ]
    payload = jnp.concatenate(
        slave_part
        + [mortar[...] * live, face[...].astype(F32), jnp.zeros((39, segs), F32)],
        axis=0,
    )
    hits = lax.broadcasted_iota(jnp.int32, (n_dom, segs), 0) == part[...]
    hits_b = jnp.where(hits, 1.0, 0.0).astype(BF16)
    earlier = (
        lax.broadcasted_iota(jnp.int32, (segs, segs), 0)
        < lax.broadcasted_iota(jnp.int32, (segs, segs), 1)
    )
    before = jnp.dot(
        hits_b, jnp.where(earlier, 1.0, 0.0).astype(BF16), preferred_element_type=F32
    )
    rank = jnp.sum(jnp.where(hits, before, 0.0), axis=0, keepdims=True).astype(jnp.int32)
    slot = part[...] * cap + rank
    slot_out[...] = slot
    place = jnp.where(
        lax.broadcasted_iota(jnp.int32, (width, segs), 0) == slot, 1.0, 0.0
    ).astype(BF16)
    p1 = payload.astype(BF16)
    rest = payload - p1.astype(F32)
    p2 = rest.astype(BF16)
    p3 = (rest - p2.astype(F32)).astype(BF16)
    out[...] = lax.dot_general(
        jnp.concatenate([place, place, place], axis=1),
        jnp.concatenate([p1, p2, p3], axis=1),
        (((1,), (1,)), ((), ())),
        preferred_element_type=F32,
    )


def master_kernel(incoming, table, faces, mult_out, force_out, nodes_out):
    own = table.shape[0] // 3
    width = incoming.shape[0]
    n_dom = width // 8
    packed = table[...]
    got = incoming[...].T
    face = got[88:89, :].astype(jnp.int32)
    groups = faces.shape[1] // LO
    listing = jnp.concatenate([faces[:, g * LO : (g + 1) * LO] for g in range(groups)], axis=0)
    f_first = (listing >> 7).astype(F32).astype(BF16)
    f_second = (listing & 127).astype(F32).astype(BF16)
    hot = one_hot_lo(face)
    f_table = jnp.concatenate([f_first, f_second], axis=0)
    picked = jnp.dot(f_table, hot, preferred_element_type=F32)
    both = picked[: 8 * groups] * 128.0 + picked[8 * groups :]
    face_hi = face >> 8
    nodes = jnp.zeros((8, width), F32)
    for g in range(groups):
        nodes = nodes + jnp.where(face_hi == g, both[8 * g : 8 * (g + 1)], 0.0)
    nodes = nodes.astype(jnp.int32)
    nodes_out[...] = nodes
    vals = [gather_column(packed, nodes[j : j + 1, :], own) for j in range(8)]
    matrix = [got[24 + 8 * i : 32 + 8 * i, :] for i in range(8)]
    mults = []
    for c in range(3):
        master = jnp.concatenate([vals[j][c] for j in range(8)], axis=0)
        force = jnp.zeros((8, width), F32)
        for i in range(8):
            gap = got[8 * c + i : 8 * c + i + 1, :] - jnp.sum(
                matrix[i] * master, axis=0, keepdims=True
            )
            mult = penalty * gap
            mults.append(mult)
            force = force - matrix[i] * mult
        force_out[8 * c : 8 * c + 8, :] = force
    back = jnp.concatenate(mults + [jnp.zeros((8, width), F32)], axis=0).T
    back = back.reshape(n_dom, 8, 32)
    for k in range(8):
        mult_out[:, 0, 32 * k : 32 * (k + 1)] = back[:, k, :]


def master_scatter_kernel(force, nodes, out):
    own = out.shape[0] // 3
    total = jnp.zeros(out.shape, F32)
    for j in range(8):
        values = [force[8 * c + j : 8 * c + j + 1, :] for c in range(3)]
        total = total + scatter_column(values, nodes[j : j + 1, :], own)
    out[...] = total


def slave_kernel(returned, slot, dual, slave, owned, master, upper, lower, out):
    own = owned.shape[0] // 3
    ghost = upper.shape[0] // 3
    segs = slot.shape[1]
    n_dom = returned.shape[0]
    mult_rows = returned[...].reshape(n_dom, 256).T
    m1 = mult_rows.astype(BF16)
    rest = mult_rows - m1.astype(F32)
    m2 = rest.astype(BF16)
    m3 = (rest - m2.astype(F32)).astype(BF16)
    hot = jnp.where(
        lax.broadcasted_iota(jnp.int32, (n_dom, segs), 0) == (slot[...] >> 3), 1.0, 0.0
    ).astype(BF16)
    picked = jnp.dot(
        jnp.concatenate([m1, m2, m3], axis=1),
        jnp.concatenate([hot, hot, hot], axis=0),
        preferred_element_type=F32,
    )
    rank = slot[...] & 7
    mult = jnp.zeros((32, segs), F32)
    for k in range(8):
        mult = mult + jnp.where(rank == k, picked[32 * k : 32 * (k + 1)], 0.0)
    total = owned[...] + master[...]
    for i in range(8):
        values = [dual[i : i + 1, :] * mult[8 * c + i : 8 * c + i + 1, :] for c in range(3)]
        total = total + scatter_column(values, slave[i : i + 1, :], own)
    quarters = out.shape[0]
    per = own // quarters
    for c in range(3):
        block = total[c * own : (c + 1) * own]
        for q in range(quarters):
            part = block[q * per : (q + 1) * per]
            if q == 0:
                part = jnp.concatenate(
                    [part[:ghost] + lower[c * ghost : (c + 1) * ghost, :], part[ghost:]], axis=0
                )
            if q == quarters - 1:
                part = jnp.concatenate(
                    [part[:-ghost], part[-ghost:] + upper[c * ghost : (c + 1) * ghost, :]], axis=0
                )
            out[q, c * per : (c + 1) * per, :] = part


def finish_kernel(own_part, a, b, d, out):
    per = own_part.shape[0] // 3
    total = own_part[...] + a[...] + b[...] + d[...]
    for c in range(3):
        for h in range(per):
            out[c : c + 1, h * LO : (h + 1) * LO] = total[c * per + h : c * per + h + 1, :]


def call(kernel, outs, *args, scratch=(), smem=(), hbm=(), flops=10**8):
    specs = [
        pl.BlockSpec(
            memory_space=pltpu.SMEM if i in smem else pltpu.HBM if i in hbm else pltpu.VMEM
        )
        for i in range(len(args))
    ]
    moved = sum(a.size * 4 for a in args)
    many = isinstance(outs, list)
    return pl.pallas_call(
        kernel,
        out_shape=outs,
        in_specs=specs,
        out_specs=[pl.BlockSpec(memory_space=pltpu.VMEM)] * len(outs)
        if many
        else pl.BlockSpec(memory_space=pltpu.VMEM),
        scratch_shapes=list(scratch),
        cost_estimate=pl.CostEstimate(flops=flops, transcendentals=0, bytes_accessed=moved),
        compiler_params=pltpu.CompilerParams(vmem_limit_bytes=48 * 1024 * 1024),
    )(*[pltpu.with_memory_space_constraint(a, pltpu.HBM) if i in hbm else a for i, a in enumerate(args)])


def shape(*dims):
    return jax.ShapeDtypeStruct(dims, F32)


def element_forces(table, before, after, connect, shear, bulk, k_shear, k_bulk):
    rows = table.shape[0] + before.shape[0] + after.shape[0]
    elems = connect.shape[1]
    return call(
        forces_kernel,
        shape(64, elems),
        table,
        before,
        after,
        connect,
        shear[None],
        bulk[None],
        k_shear,
        k_bulk,
        scratch=[
            pltpu.VMEM((rows, 2 * LO), BF16),
            pltpu.VMEM((64, elems), F32),
            pltpu.VMEM((64, 64), F32),
        ],
        flops=8 * 10**9,
    )


def element_scatter(forces, connect, nodes):
    own = nodes // LO
    ghost = GHOST // LO
    return call(
        element_scatter_kernel,
        [shape(3 * own, LO), shape(3 * ghost, LO), shape(3 * ghost, LO)],
        forces,
        connect,
        scratch=[pltpu.VMEM((3 * (own + 2 * ghost), LO), F32)],
        flops=8 * 10**9,
    )


def pack(displacement, seg_slave, dual, mortar, seg_face, seg_part, seg_count, n_dom):
    own = displacement.shape[1] // LO
    segs = seg_face.shape[0]
    return call(
        pack_kernel,
        [
            shape(n_dom * 8, 128),
            jax.ShapeDtypeStruct((1, segs), jnp.int32),
            jax.ShapeDtypeStruct((3 * own, 2 * LO), BF16),
            shape(3 * GHOST // LO, LO),
            shape(3 * GHOST // LO, LO),
        ],
        displacement,
        seg_slave,
        dual,
        mortar,
        seg_face[None],
        seg_part.reshape(1, segs),
        seg_count.reshape(1, 1),
        smem=(6,),
        hbm=(0, 1, 2, 3, 4, 5),
        scratch=[
            pltpu.VMEM((3 * own, LO), F32),
            pltpu.VMEM(displacement.shape, F32),
            pltpu.VMEM(seg_slave.shape, jnp.int32),
            pltpu.VMEM(dual.shape, F32),
            pltpu.VMEM(mortar.shape, F32),
            pltpu.VMEM((1, segs), jnp.int32),
            pltpu.VMEM((1, segs), jnp.int32),
            pltpu.SemaphoreType.DMA((6,)),
        ],
    )


def master(incoming, table, face_nodes):
    width = incoming.shape[0]
    return call(
        master_kernel,
        [
            shape(width // 8, 1, 256),
            shape(24, width),
            jax.ShapeDtypeStruct((8, width), jnp.int32),
        ],
        incoming,
        table,
        face_nodes,
    )


def slave_side(returned, slot, dual, seg_slave, owned, master_part, upper, lower, n_sub):
    own = owned.shape[0] // 3
    return call(
        slave_kernel,
        shape(n_sub, 3 * own // n_sub, LO),
        returned,
        slot,
        dual,
        seg_slave,
        owned,
        master_part,
        upper,
        lower,
    )


def on_device(
    displacement,
    connect,
    shear,
    bulk,
    stiff_shear,
    stiff_bulk,
    seg_slave,
    seg_part,
    seg_face,
    face_nodes,
    dual,
    mortar,
    seg_count,
):
    nodes = displacement.shape[1]
    n_dom, n_sub = lax.axis_size("dom"), lax.axis_size("sub")
    up = [(i, i + 1) for i in range(n_dom - 1)]
    down = [(i + 1, i) for i in range(n_dom - 1)]
    outgoing, slot, table, head, tail = pack(
        displacement, seg_slave, dual, mortar, seg_face, seg_part, seg_count, n_dom
    )
    incoming = lax.all_to_all(
        outgoing.reshape(n_dom, 8, 128), "dom", split_axis=0, concat_axis=0, tiled=True
    )
    before = lax.ppermute(tail, "dom", up)
    after = lax.ppermute(head, "dom", down)
    forces = element_forces(table, before, after, connect, shear, bulk, stiff_shear, stiff_bulk)
    incoming, forces = lax.optimization_barrier((incoming, forces))
    mult, master_force, master_nodes = master(
        incoming.reshape(n_dom * 8, 128), table, face_nodes
    )
    returned = lax.all_to_all(mult, "dom", split_axis=0, concat_axis=0, tiled=True)
    forces, _ = lax.optimization_barrier((forces, mult))
    owned, low, high = element_scatter(forces, connect, nodes)
    upper = lax.ppermute(low, "dom", down)
    lower = lax.ppermute(high, "dom", up)
    master_part = call(
        master_scatter_kernel, shape(3 * nodes // LO, LO), master_force, master_nodes
    )
    blocks = slave_side(
        returned, slot, dual, seg_slave, owned, master_part, upper, lower, n_sub
    )
    me = lax.axis_index("sub")
    sent = [
        lax.ppermute(
            lax.dynamic_index_in_dim(blocks, (me + k) % n_sub, 0, keepdims=False),
            "sub",
            [(s, (s + k) % n_sub) for s in range(n_sub)],
        )
        for k in range(1, n_sub)
    ]
    mine = lax.dynamic_index_in_dim(blocks, me, 0, keepdims=False)
    return call(finish_kernel, shape(3, nodes // n_sub), mine, *sent)


def solution(mesh):
    placed = (
        P(None, "dom"),
        P(None, ("dom", "sub")),
        P(("dom", "sub")),
        P(("dom", "sub")),
        P(),
        P(),
        P(None, ("dom", "sub")),
        P(("dom", "sub"), None),
        P(("dom", "sub")),
        P(None, "dom"),
        P(None, ("dom", "sub")),
        P(None, ("dom", "sub")),
        P(("dom", "sub")),
    )
    return jax.shard_map(
        on_device, mesh=mesh, in_specs=placed, out_specs=P(None, ("dom", "sub")), check_vma=False
    )
```

```python
import jax
import jax.numpy as jnp
from jax import lax
from jax.experimental import pallas as pl
from jax.experimental.pallas import tpu as pltpu
from jax.sharding import PartitionSpec as P

GHOST = 2048
LO = 256
penalty = 2.0
ELEMENT_FLOPS = 8 * 10**9
F32 = jnp.float32
BF16 = jnp.bfloat16


def pieces(x):
    first = x.astype(BF16)
    second = (x - first.astype(F32)).astype(BF16)
    return first, second


def one_hot_lo(index):
    n = index.shape[1]
    rows = lax.broadcasted_iota(jnp.int16, (LO, n), 0)
    low = (index & (LO - 1)).astype(jnp.int16)
    return jnp.where(rows == low, jnp.bfloat16(1), jnp.bfloat16(0))


def hi_mask(index, rows):
    n = index.shape[1]
    return lax.broadcasted_iota(jnp.int32, (rows, n), 0) == (index >> 8)


def to_rows(source, offset, count, target, first_row, stride):
    for c in range(3):
        for h in range(count):
            row = c * stride + first_row + h
            target[row : row + 1, :] = source[c : c + 1, offset + h * LO : offset + (h + 1) * LO]


def gather_column(table, hot, mask):
    rows = mask.shape[0]
    picked = jnp.dot(table, jnp.concatenate([hot, hot], axis=0), preferred_element_type=F32)
    return [
        jnp.sum(jnp.where(mask, picked[c * rows : (c + 1) * rows], 0.0), axis=0, keepdims=True)
        for c in range(3)
    ]


def scatter_column(values, hot, mask):
    firsts, seconds = [], []
    for c in range(3):
        first, second = pieces(values[c])
        firsts.append(jnp.where(mask, first.astype(F32), 0.0).astype(BF16))
        seconds.append(jnp.where(mask, second.astype(F32), 0.0).astype(BF16))
    spread = jnp.concatenate(
        [jnp.concatenate(firsts, axis=0), jnp.concatenate(seconds, axis=0)], axis=1
    )
    return lax.dot_general(
        spread,
        jnp.concatenate([hot, hot], axis=1),
        (((1,), (1,)), ((), ())),
        preferred_element_type=F32,
    )


def gather(table, index, rows):
    return gather_column(table, one_hot_lo(index), hi_mask(index, rows))


def scatter(values, index, rows):
    return scatter_column(values, one_hot_lo(index), hi_mask(index, rows))


def by_side(near, far):
    here_dom, n_dom = lax.axis_index("dom"), lax.axis_size("dom")
    even = here_dom % 2 == 0
    below = jnp.where(here_dom == 0, 0.0, jnp.where(even, far, near))
    above = jnp.where(here_dom == n_dom - 1, 0.0, jnp.where(even, near, far))
    return below, above


def element_kernel(
    own, near, far, connect, shear, bulk, k_shear, k_bulk,
    owned, near_out, far_out, table, dofs, k_pad, hots, total,
):
    ghost = near.shape[0] // 3
    count = own.shape[0] // 3
    rows = count + 2 * ghost
    for source, first_row in zip(by_side(near[...], far[...]), (0, rows - ghost)):
        first, second = pieces(source)
        for c in range(3):
            here = slice(c * rows + first_row, c * rows + first_row + ghost)
            table[here, :LO] = first[c * ghost : (c + 1) * ghost]
            table[here, LO:] = second[c * ghost : (c + 1) * ghost]
    for c in range(3):
        table[c * rows + ghost : c * rows + ghost + count, :] = own[c * count : (c + 1) * count, :]
    dofs[...] = jnp.zeros_like(dofs)
    for a in range(20):
        index = connect[a : a + 1, :]
        hot = one_hot_lo(index)
        hots[a] = hot
        got = gather_column(table[...], hot, hi_mask(index, rows))
        for c in range(3):
            dofs[20 * c + a : 20 * c + a + 1, :] = got[c]
    g_first, g_second = pieces(dofs[...])
    g = jnp.concatenate([g_first, g_first, g_second, g_second], axis=0)

    def product(k):
        k_pad[...] = jnp.zeros_like(k_pad)
        k_pad[: k.shape[0], : k.shape[1]] = k[...]
        k_first, k_second = pieces(k_pad[...].T)
        wide = jnp.concatenate([k_first, k_second, k_first, k_second], axis=1)
        return jnp.dot(wide, g, preferred_element_type=F32)

    dofs[...] = shear[...] * product(k_shear) + bulk[...] * product(k_bulk)
    total[...] = jnp.zeros_like(total)
    for a in range(20):
        values = [dofs[20 * c + a : 20 * c + a + 1, :] for c in range(3)]
        total[...] += scatter_column(values, hots[a], hi_mask(connect[a : a + 1, :], rows))
    even = lax.axis_index("dom") % 2 == 0
    for c in range(3):
        base = c * rows
        here = slice(c * ghost, (c + 1) * ghost)
        low = total[base : base + ghost, :]
        high = total[base + ghost + count : base + rows, :]
        near_out[here, :] = jnp.where(even, high, low)
        far_out[here, :] = jnp.where(even, low, high)
        owned[c * count : (c + 1) * count, :] = total[base + ghost : base + ghost + count, :]


def pack_kernel(*refs):
    given, (count, out, slot_out, table, near, far, rows) = refs[:6], refs[6:13]
    held, sems = refs[13:19], refs[19]
    copies = [pltpu.make_async_copy(a, b, sems.at[i]) for i, (a, b) in enumerate(zip(given, held))]
    for copy in copies:
        copy.start()
    for copy in copies:
        copy.wait()
    disp, slave, dual, mortar, face, part = held
    segs = slave.shape[1]
    own = disp.shape[1] // LO
    to_rows(disp, 0, own, rows, 0, own)
    first, second = pieces(rows[...])
    packed = jnp.concatenate([first, second], axis=1)
    table[...] = packed
    ghost = GHOST // LO
    even = lax.axis_index("dom") % 2 == 0
    for c in range(3):
        head = rows[c * own : c * own + ghost, :]
        tail = rows[(c + 1) * own - ghost : (c + 1) * own, :]
        near[c * ghost : (c + 1) * ghost, :] = jnp.where(even, tail, head)
        far[c * ghost : (c + 1) * ghost, :] = jnp.where(even, head, tail)
    cap = 8
    width = out.shape[0]
    n_dom = width // cap
    lanes = lax.broadcasted_iota(jnp.int32, (1, segs), 1)
    live = jnp.where(lanes < count[0, 0], 1.0, 0.0)
    vals = []
    for i in range(8):
        vals.append(gather(packed, slave[i : i + 1, :], own))
    slave_part = [
        (dual[i : i + 1, :] * live) * vals[i][c] for c in range(3) for i in range(8)
    ]
    payload = jnp.concatenate(
        slave_part
        + [mortar[...] * live, face[...].astype(F32), jnp.zeros((39, segs), F32)],
        axis=0,
    )
    hits = lax.broadcasted_iota(jnp.int32, (n_dom, segs), 0) == part[...]
    hits_b = jnp.where(hits, 1.0, 0.0).astype(BF16)
    earlier = (
        lax.broadcasted_iota(jnp.int32, (segs, segs), 0)
        < lax.broadcasted_iota(jnp.int32, (segs, segs), 1)
    )
    before = jnp.dot(
        hits_b, jnp.where(earlier, 1.0, 0.0).astype(BF16), preferred_element_type=F32
    )
    rank = jnp.sum(jnp.where(hits, before, 0.0), axis=0, keepdims=True).astype(jnp.int32)
    slot = part[...] * cap + rank
    slot_out[...] = slot
    place = jnp.where(
        lax.broadcasted_iota(jnp.int32, (width, segs), 0) == slot, 1.0, 0.0
    ).astype(BF16)
    p1 = payload.astype(BF16)
    rest = payload - p1.astype(F32)
    p2 = rest.astype(BF16)
    p3 = (rest - p2.astype(F32)).astype(BF16)
    out[...] = lax.dot_general(
        jnp.concatenate([place, place, place], axis=1),
        jnp.concatenate([p1, p2, p3], axis=1),
        (((1,), (1,)), ((), ())),
        preferred_element_type=F32,
    )


def master_kernel(incoming, table, faces, mult_out, force_out, nodes_out):
    own = table.shape[0] // 3
    width = incoming.shape[0]
    n_dom = width // 8
    packed = table[...]
    got = incoming[...].T
    face = got[88:89, :].astype(jnp.int32)
    groups = faces.shape[1] // LO
    listing = jnp.concatenate([faces[:, g * LO : (g + 1) * LO] for g in range(groups)], axis=0)
    f_first = (listing >> 7).astype(F32).astype(BF16)
    f_second = (listing & 127).astype(F32).astype(BF16)
    hot = one_hot_lo(face)
    f_table = jnp.concatenate([f_first, f_second], axis=0)
    picked = jnp.dot(f_table, hot, preferred_element_type=F32)
    both = picked[: 8 * groups] * 128.0 + picked[8 * groups :]
    face_hi = face >> 8
    nodes = jnp.zeros((8, width), F32)
    for g in range(groups):
        nodes = nodes + jnp.where(face_hi == g, both[8 * g : 8 * (g + 1)], 0.0)
    nodes = nodes.astype(jnp.int32)
    nodes_out[...] = nodes
    vals = [gather(packed, nodes[j : j + 1, :], own) for j in range(8)]
    matrix = [got[24 + 8 * i : 32 + 8 * i, :] for i in range(8)]
    mults = []
    for c in range(3):
        master = jnp.concatenate([vals[j][c] for j in range(8)], axis=0)
        force = jnp.zeros((8, width), F32)
        for i in range(8):
            gap = got[8 * c + i : 8 * c + i + 1, :] - jnp.sum(
                matrix[i] * master, axis=0, keepdims=True
            )
            mult = penalty * gap
            mults.append(mult)
            force = force - matrix[i] * mult
        force_out[8 * c : 8 * c + 8, :] = force
    back = jnp.concatenate(mults + [jnp.zeros((8, width), F32)], axis=0).T
    back = back.reshape(n_dom, 8, 32)
    for k in range(8):
        mult_out[:, 0, 32 * k : 32 * (k + 1)] = back[:, k, :]


def master_scatter_kernel(force, nodes, out):
    own = out.shape[0] // 3
    total = jnp.zeros(out.shape, F32)
    for j in range(8):
        values = [force[8 * c + j : 8 * c + j + 1, :] for c in range(3)]
        total = total + scatter(values, nodes[j : j + 1, :], own)
    out[...] = total


def slave_kernel(returned, slot, dual, slave, owned, master, near, far, out):
    lower, upper = by_side(near[...], far[...])
    own = owned.shape[0] // 3
    ghost = near.shape[0] // 3
    segs = slot.shape[1]
    n_dom = returned.shape[0]
    mult_rows = returned[...].reshape(n_dom, 256).T
    m1 = mult_rows.astype(BF16)
    rest = mult_rows - m1.astype(F32)
    m2 = rest.astype(BF16)
    m3 = (rest - m2.astype(F32)).astype(BF16)
    hot = jnp.where(
        lax.broadcasted_iota(jnp.int32, (n_dom, segs), 0) == (slot[...] >> 3), 1.0, 0.0
    ).astype(BF16)
    picked = jnp.dot(
        jnp.concatenate([m1, m2, m3], axis=1),
        jnp.concatenate([hot, hot, hot], axis=0),
        preferred_element_type=F32,
    )
    rank = slot[...] & 7
    mult = jnp.zeros((32, segs), F32)
    for k in range(8):
        mult = mult + jnp.where(rank == k, picked[32 * k : 32 * (k + 1)], 0.0)
    total = owned[...] + master[...]
    for i in range(8):
        values = [dual[i : i + 1, :] * mult[8 * c + i : 8 * c + i + 1, :] for c in range(3)]
        total = total + scatter(values, slave[i : i + 1, :], own)
    quarters = out.shape[0]
    per = own // quarters
    for c in range(3):
        block = total[c * own : (c + 1) * own]
        for q in range(quarters):
            part = block[q * per : (q + 1) * per]
            if q == 0:
                part = jnp.concatenate(
                    [part[:ghost] + lower[c * ghost : (c + 1) * ghost], part[ghost:]], axis=0
                )
            if q == quarters - 1:
                part = jnp.concatenate(
                    [part[:-ghost], part[-ghost:] + upper[c * ghost : (c + 1) * ghost]], axis=0
                )
            out[q, c * per : (c + 1) * per, :] = part


def finish_kernel(own_part, a, b, d, out):
    per = own_part.shape[0] // 3
    total = own_part[...] + a[...] + b[...] + d[...]
    for c in range(3):
        for h in range(per):
            out[c : c + 1, h * LO : (h + 1) * LO] = total[c * per + h : c * per + h + 1, :]


def call(kernel, outs, *args, scratch=(), smem=(), hbm=(), flops=10**8):
    specs = [
        pl.BlockSpec(
            memory_space=pltpu.SMEM if i in smem else pltpu.HBM if i in hbm else pltpu.VMEM
        )
        for i in range(len(args))
    ]
    moved = sum(a.size * 4 for a in args)
    many = isinstance(outs, list)
    return pl.pallas_call(
        kernel,
        out_shape=outs,
        in_specs=specs,
        out_specs=[pl.BlockSpec(memory_space=pltpu.VMEM)] * len(outs)
        if many
        else pl.BlockSpec(memory_space=pltpu.VMEM),
        scratch_shapes=list(scratch),
        cost_estimate=pl.CostEstimate(flops=flops, transcendentals=0, bytes_accessed=moved),
        compiler_params=pltpu.CompilerParams(vmem_limit_bytes=48 * 1024 * 1024),
    )(*[pltpu.with_memory_space_constraint(a, pltpu.HBM) if i in hbm else a for i, a in enumerate(args)])


def shape(*dims):
    return jax.ShapeDtypeStruct(dims, F32)


def elements(table, near, far, connect, shear, bulk, k_shear, k_bulk):
    rows = table.shape[0] + near.shape[0] + far.shape[0]
    elems = connect.shape[1]
    return call(
        element_kernel,
        [shape(table.shape[0], LO), shape(*near.shape), shape(*far.shape)],
        table,
        near,
        far,
        connect,
        shear[None],
        bulk[None],
        k_shear,
        k_bulk,
        scratch=[
            pltpu.VMEM((rows, 2 * LO), BF16),
            pltpu.VMEM((64, elems), F32),
            pltpu.VMEM((64, 64), F32),
            pltpu.VMEM((20, LO, elems), BF16),
            pltpu.VMEM((rows, LO), F32),
        ],
        flops=ELEMENT_FLOPS,
    )


def pack(displacement, seg_slave, dual, mortar, seg_face, seg_part, seg_count, n_dom):
    own = displacement.shape[1] // LO
    segs = seg_face.shape[0]
    return call(
        pack_kernel,
        [
            shape(n_dom * 8, 128),
            jax.ShapeDtypeStruct((1, segs), jnp.int32),
            jax.ShapeDtypeStruct((3 * own, 2 * LO), BF16),
            shape(3 * GHOST // LO, LO),
            shape(3 * GHOST // LO, LO),
        ],
        displacement,
        seg_slave,
        dual,
        mortar,
        seg_face[None],
        seg_part.reshape(1, segs),
        seg_count.reshape(1, 1),
        smem=(6,),
        hbm=(0, 1, 2, 3, 4, 5),
        scratch=[
            pltpu.VMEM((3 * own, LO), F32),
            pltpu.VMEM(displacement.shape, F32),
            pltpu.VMEM(seg_slave.shape, jnp.int32),
            pltpu.VMEM(dual.shape, F32),
            pltpu.VMEM(mortar.shape, F32),
            pltpu.VMEM((1, segs), jnp.int32),
            pltpu.VMEM((1, segs), jnp.int32),
            pltpu.SemaphoreType.DMA((6,)),
        ],
    )


def master(incoming, table, face_nodes):
    width = incoming.shape[0]
    return call(
        master_kernel,
        [
            shape(width // 8, 1, 256),
            shape(24, width),
            jax.ShapeDtypeStruct((8, width), jnp.int32),
        ],
        incoming,
        table,
        face_nodes,
    )


def slave_side(returned, slot, dual, seg_slave, owned, master_part, near, far, n_sub):
    own = owned.shape[0] // 3
    return call(
        slave_kernel,
        shape(n_sub, 3 * own // n_sub, LO),
        returned,
        slot,
        dual,
        seg_slave,
        owned,
        master_part,
        near,
        far,
    )


def on_device(
    displacement,
    connect,
    shear,
    bulk,
    stiff_shear,
    stiff_bulk,
    seg_slave,
    seg_part,
    seg_face,
    face_nodes,
    dual,
    mortar,
    seg_count,
):
    nodes = displacement.shape[1]
    n_dom, n_sub = lax.axis_size("dom"), lax.axis_size("sub")
    near_pairs = [(i, i ^ 1) for i in range(n_dom)]
    far_pairs = [(i, min(max(((i + 1) ^ 1) - 1, 0), n_dom - 1)) for i in range(n_dom)]
    outgoing, slot, table, near, far = pack(
        displacement, seg_slave, dual, mortar, seg_face, seg_part, seg_count, n_dom
    )
    incoming = lax.all_to_all(
        outgoing.reshape(n_dom, 8, 128), "dom", split_axis=0, concat_axis=0, tiled=True
    )
    near = lax.ppermute(near, "dom", near_pairs)
    far = lax.ppermute(far, "dom", far_pairs)
    owned, near, far = elements(
        table, near, far, connect, shear, bulk, stiff_shear, stiff_bulk
    )
    incoming, owned = lax.optimization_barrier((incoming, owned))
    mult, master_force, master_nodes = master(
        incoming.reshape(n_dom * 8, 128), table, face_nodes
    )
    returned = lax.all_to_all(mult, "dom", split_axis=0, concat_axis=0, tiled=True)
    near = lax.ppermute(near, "dom", near_pairs)
    far = lax.ppermute(far, "dom", far_pairs)
    master_part = call(
        master_scatter_kernel, shape(3 * nodes // LO, LO), master_force, master_nodes
    )
    blocks = slave_side(
        returned, slot, dual, seg_slave, owned, master_part, near, far, n_sub
    )
    me = lax.axis_index("sub")
    sent = [
        lax.ppermute(
            lax.dynamic_index_in_dim(blocks, (me + k) % n_sub, 0, keepdims=False),
            "sub",
            [(s, (s + k) % n_sub) for s in range(n_sub)],
        )
        for k in range(1, n_sub)
    ]
    mine = lax.dynamic_index_in_dim(blocks, me, 0, keepdims=False)
    return call(finish_kernel, shape(3, nodes // n_sub), mine, *sent)


def solution(mesh):
    placed = (
        P(None, "dom"),
        P(None, ("dom", "sub")),
        P(("dom", "sub")),
        P(("dom", "sub")),
        P(),
        P(),
        P(None, ("dom", "sub")),
        P(("dom", "sub"), None),
        P(("dom", "sub")),
        P(None, "dom"),
        P(None, ("dom", "sub")),
        P(None, ("dom", "sub")),
        P(("dom", "sub")),
    )
    return jax.shard_map(
        on_device, mesh=mesh, in_specs=placed, out_specs=P(None, ("dom", "sub")), check_vma=False
    )
```

```python
import jax
import jax.numpy as jnp
from jax import lax
from jax.experimental import pallas as pl
from jax.experimental.pallas import tpu as pltpu
from jax.sharding import PartitionSpec as P

GHOST = 2048
LO = 256
penalty = 2.0
WORDS = 96
ELEMENT_FLOPS = 8 * 10**9
F32 = jnp.float32
BF16 = jnp.bfloat16


def pieces(x):
    first = x.astype(BF16)
    second = (x - first.astype(F32)).astype(BF16)
    return first, second


def one_hot_lo(index):
    n = index.shape[1]
    rows = lax.broadcasted_iota(jnp.int16, (LO, n), 0)
    low = (index & (LO - 1)).astype(jnp.int16)
    return jnp.where(rows == low, jnp.bfloat16(1), jnp.bfloat16(0))


def hi_mask(index, rows):
    n = index.shape[1]
    return lax.broadcasted_iota(jnp.int32, (rows, n), 0) == (index >> 8)


def to_rows(source, offset, count, target, first_row, stride):
    for c in range(3):
        for h in range(count):
            row = c * stride + first_row + h
            target[row : row + 1, :] = source[c : c + 1, offset + h * LO : offset + (h + 1) * LO]


def gather_column(table, hot, mask):
    rows = mask.shape[0]
    picked = jnp.dot(table, jnp.concatenate([hot, hot], axis=0), preferred_element_type=F32)
    return [
        jnp.sum(jnp.where(mask, picked[c * rows : (c + 1) * rows], 0.0), axis=0, keepdims=True)
        for c in range(3)
    ]


def scatter_column(values, hot, mask):
    firsts, seconds = [], []
    for c in range(3):
        first, second = pieces(values[c])
        firsts.append(jnp.where(mask, first.astype(F32), 0.0).astype(BF16))
        seconds.append(jnp.where(mask, second.astype(F32), 0.0).astype(BF16))
    spread = jnp.concatenate(
        [jnp.concatenate(firsts, axis=0), jnp.concatenate(seconds, axis=0)], axis=1
    )
    return lax.dot_general(
        spread,
        jnp.concatenate([hot, hot], axis=1),
        (((1,), (1,)), ((), ())),
        preferred_element_type=F32,
    )


def gather(table, index, rows):
    return gather_column(table, one_hot_lo(index), hi_mask(index, rows))


def scatter(values, index, rows):
    return scatter_column(values, one_hot_lo(index), hi_mask(index, rows))


def by_side(near, far):
    here_dom, n_dom = lax.axis_index("dom"), lax.axis_size("dom")
    even = here_dom % 2 == 0
    below = jnp.where(here_dom == 0, 0.0, jnp.where(even, far, near))
    above = jnp.where(here_dom == n_dom - 1, 0.0, jnp.where(even, near, far))
    return below, above


def element_kernel(
    own, near, far, connect, shear, bulk, k_shear, k_bulk,
    owned, near_out, far_out, table, dofs, k_pad, hots, total,
):
    ghost = near.shape[0] // 3
    count = own.shape[0] // 3
    rows = count + 2 * ghost
    elems = connect.shape[1]
    for source, first_row in zip(by_side(near[...], far[...]), (0, rows - ghost)):
        first, second = pieces(source)
        for c in range(3):
            here = slice(c * rows + first_row, c * rows + first_row + ghost)
            table[here, :LO] = first[c * ghost : (c + 1) * ghost]
            table[here, LO:] = second[c * ghost : (c + 1) * ghost]
    for c in range(3):
        table[c * rows + ghost : c * rows + ghost + count, :] = own[c * count : (c + 1) * count, :]
    dofs[...] = jnp.zeros_like(dofs)
    for a in range(20):
        index = connect[a : a + 1, :]
        hot = one_hot_lo(index)
        hots[a] = hot
        got = gather_column(table[...], hot, hi_mask(index, rows))
        for c in range(3):
            dofs[20 * c + a : 20 * c + a + 1, :] = got[c]
    g_first, g_second = pieces(dofs[...])
    g = jnp.concatenate([g_first, g_first, g_second, g_second], axis=0)

    def product(k):
        k_pad[...] = jnp.zeros_like(k_pad)
        k_pad[: k.shape[0], : k.shape[1]] = k[...]
        k_first, k_second = pieces(k_pad[...].T)
        wide = jnp.concatenate([k_first, k_second, k_first, k_second], axis=1)
        return jnp.dot(wide, g, preferred_element_type=F32)

    by_shear, by_bulk = (m[...].reshape(1, elems) for m in (shear, bulk))
    dofs[...] = by_shear * product(k_shear) + by_bulk * product(k_bulk)
    total[...] = jnp.zeros_like(total)
    for a in range(20):
        values = [dofs[20 * c + a : 20 * c + a + 1, :] for c in range(3)]
        total[...] += scatter_column(values, hots[a], hi_mask(connect[a : a + 1, :], rows))
    even = lax.axis_index("dom") % 2 == 0
    for c in range(3):
        base = c * rows
        here = slice(c * ghost, (c + 1) * ghost)
        low = total[base : base + ghost, :]
        high = total[base + ghost + count : base + rows, :]
        near_out[here, :] = jnp.where(even, high, low)
        far_out[here, :] = jnp.where(even, low, high)
        owned[c * count : (c + 1) * count, :] = total[base + ghost : base + ghost + count, :]


def place_in_group(part, n_dom):
    ny, nz = 4, n_dom // 8
    y, z, core = part // (2 * nz), (part // 2) % nz, part % 2
    return n_dom - 1 - (z * (2 * ny) + y * 2 + core)


def pack_kernel(*refs):
    given, (count, out, slot_out, table, near, far, rows) = refs[:6], refs[6:13]
    held, sems = refs[13:19], refs[19]
    copies = [pltpu.make_async_copy(a, b, sems.at[i]) for i, (a, b) in enumerate(zip(given, held))]
    for copy in copies:
        copy.start()
    for copy in copies:
        copy.wait()
    disp, slave, dual, mortar, face, part = held
    segs = slave.shape[1]
    own = disp.shape[1] // LO
    to_rows(disp, 0, own, rows, 0, own)
    first, second = pieces(rows[...])
    packed = jnp.concatenate([first, second], axis=1)
    table[...] = packed
    ghost = GHOST // LO
    even = lax.axis_index("dom") % 2 == 0
    for c in range(3):
        head = rows[c * own : c * own + ghost, :]
        tail = rows[(c + 1) * own - ghost : (c + 1) * own, :]
        near[c * ghost : (c + 1) * ghost, :] = jnp.where(even, tail, head)
        far[c * ghost : (c + 1) * ghost, :] = jnp.where(even, head, tail)
    cap = 8
    n_dom = out.shape[0]
    width = n_dom * cap
    lanes = lax.broadcasted_iota(jnp.int32, (1, segs), 1)
    live = jnp.where(lanes < count[0, 0], 1.0, 0.0)
    vals = []
    for i in range(8):
        vals.append(gather(packed, slave[i : i + 1, :], own))
    slave_part = [
        (dual[i : i + 1, :] * live) * vals[i][c] for c in range(3) for i in range(8)
    ]
    payload = jnp.concatenate(
        slave_part
        + [mortar[...] * live, face[...].astype(F32), jnp.zeros((WORDS - 89, segs), F32)],
        axis=0,
    )
    hits = lax.broadcasted_iota(jnp.int32, (n_dom, segs), 0) == part[...]
    hits_b = jnp.where(hits, 1.0, 0.0).astype(BF16)
    earlier = (
        lax.broadcasted_iota(jnp.int32, (segs, segs), 0)
        < lax.broadcasted_iota(jnp.int32, (segs, segs), 1)
    )
    before = jnp.dot(
        hits_b, jnp.where(earlier, 1.0, 0.0).astype(BF16), preferred_element_type=F32
    )
    rank = jnp.sum(jnp.where(hits, before, 0.0), axis=0, keepdims=True).astype(jnp.int32)
    place_of = place_in_group(part[...], n_dom)
    slot = rank * n_dom + place_of
    slot_out[0:1, :] = place_of
    slot_out[1:2, :] = rank
    place = jnp.where(
        lax.broadcasted_iota(jnp.int32, (width, segs), 0) == slot, 1.0, 0.0
    ).astype(BF16)
    p1 = payload.astype(BF16)
    rest = payload - p1.astype(F32)
    p2 = rest.astype(BF16)
    p3 = (rest - p2.astype(F32)).astype(BF16)
    placed = lax.dot_general(
        jnp.concatenate([place, place, place], axis=1),
        jnp.concatenate([p1, p2, p3], axis=1),
        (((1,), (1,)), ((), ())),
        preferred_element_type=F32,
    )
    for k in range(cap):
        out[:, 0, WORDS * k : WORDS * (k + 1)] = placed[n_dom * k : n_dom * (k + 1), :]


def master_kernel(incoming, table, faces, mult_out, force_out, nodes_out):
    own = table.shape[0] // 3
    n_dom = incoming.shape[0]
    width = n_dom * 8
    packed = table[...]
    got = jnp.concatenate(
        [incoming[:, 0, WORDS * k : WORDS * (k + 1)] for k in range(8)], axis=0
    ).T
    face = got[88:89, :].astype(jnp.int32)
    groups = faces.shape[1] // LO
    listing = jnp.concatenate([faces[:, g * LO : (g + 1) * LO] for g in range(groups)], axis=0)
    f_first = (listing >> 7).astype(F32).astype(BF16)
    f_second = (listing & 127).astype(F32).astype(BF16)
    hot = one_hot_lo(face)
    f_table = jnp.concatenate([f_first, f_second], axis=0)
    picked = jnp.dot(f_table, hot, preferred_element_type=F32)
    both = picked[: 8 * groups] * 128.0 + picked[8 * groups :]
    face_hi = face >> 8
    nodes = jnp.zeros((8, width), F32)
    for g in range(groups):
        nodes = nodes + jnp.where(face_hi == g, both[8 * g : 8 * (g + 1)], 0.0)
    nodes = nodes.astype(jnp.int32)
    nodes_out[...] = nodes
    vals = [gather(packed, nodes[j : j + 1, :], own) for j in range(8)]
    matrix = [got[24 + 8 * i : 32 + 8 * i, :] for i in range(8)]
    mults = []
    for c in range(3):
        master = jnp.concatenate([vals[j][c] for j in range(8)], axis=0)
        force = jnp.zeros((8, width), F32)
        for i in range(8):
            gap = got[8 * c + i : 8 * c + i + 1, :] - jnp.sum(
                matrix[i] * master, axis=0, keepdims=True
            )
            mult = penalty * gap
            mults.append(mult)
            force = force - matrix[i] * mult
        force_out[8 * c : 8 * c + 8, :] = force
    back = jnp.concatenate(mults + [jnp.zeros((8, width), F32)], axis=0).T
    for k in range(8):
        mult_out[:, 0, 32 * k : 32 * (k + 1)] = back[n_dom * k : n_dom * (k + 1), :]


def master_scatter_kernel(force, nodes, out):
    own = out.shape[0] // 3
    total = jnp.zeros(out.shape, F32)
    for j in range(8):
        values = [force[8 * c + j : 8 * c + j + 1, :] for c in range(3)]
        total = total + scatter(values, nodes[j : j + 1, :], own)
    out[...] = total


def slave_kernel(returned, slot, dual, slave, owned, master, near, far, out):
    lower, upper = by_side(near[...], far[...])
    own = owned.shape[0] // 3
    ghost = near.shape[0] // 3
    segs = slot.shape[1]
    n_dom = returned.shape[0]
    mult_rows = returned[...].reshape(n_dom, 256).T
    m1 = mult_rows.astype(BF16)
    rest = mult_rows - m1.astype(F32)
    m2 = rest.astype(BF16)
    m3 = (rest - m2.astype(F32)).astype(BF16)
    hot = jnp.where(
        lax.broadcasted_iota(jnp.int32, (n_dom, segs), 0) == slot[0:1, :], 1.0, 0.0
    ).astype(BF16)
    picked = jnp.dot(
        jnp.concatenate([m1, m2, m3], axis=1),
        jnp.concatenate([hot, hot, hot], axis=0),
        preferred_element_type=F32,
    )
    rank = slot[1:2, :]
    mult = jnp.zeros((32, segs), F32)
    for k in range(8):
        mult = mult + jnp.where(rank == k, picked[32 * k : 32 * (k + 1)], 0.0)
    total = owned[...] + master[...]
    for i in range(8):
        values = [dual[i : i + 1, :] * mult[8 * c + i : 8 * c + i + 1, :] for c in range(3)]
        total = total + scatter(values, slave[i : i + 1, :], own)
    quarters = out.shape[0]
    per = own // quarters
    for c in range(3):
        block = total[c * own : (c + 1) * own]
        for q in range(quarters):
            part = block[q * per : (q + 1) * per]
            if q == 0:
                part = jnp.concatenate(
                    [part[:ghost] + lower[c * ghost : (c + 1) * ghost], part[ghost:]], axis=0
                )
            if q == quarters - 1:
                part = jnp.concatenate(
                    [part[:-ghost], part[-ghost:] + upper[c * ghost : (c + 1) * ghost]], axis=0
                )
            out[q, c * per : (c + 1) * per, :] = part


def finish_kernel(own_part, a, b, d, out):
    per = own_part.shape[0] // 3
    total = own_part[...] + a[...] + b[...] + d[...]
    for c in range(3):
        for h in range(per):
            out[c : c + 1, h * LO : (h + 1) * LO] = total[c * per + h : c * per + h + 1, :]


def call(kernel, outs, *args, scratch=(), smem=(), hbm=(), flops=10**8):
    specs = [
        pl.BlockSpec(
            memory_space=pltpu.SMEM if i in smem else pltpu.HBM if i in hbm else pltpu.VMEM
        )
        for i in range(len(args))
    ]
    moved = sum(a.size * 4 for a in args)
    many = isinstance(outs, list)
    return pl.pallas_call(
        kernel,
        out_shape=outs,
        in_specs=specs,
        out_specs=[pl.BlockSpec(memory_space=pltpu.VMEM)] * len(outs)
        if many
        else pl.BlockSpec(memory_space=pltpu.VMEM),
        scratch_shapes=list(scratch),
        cost_estimate=pl.CostEstimate(flops=flops, transcendentals=0, bytes_accessed=moved),
        compiler_params=pltpu.CompilerParams(vmem_limit_bytes=48 * 1024 * 1024),
    )(*[pltpu.with_memory_space_constraint(a, pltpu.HBM) if i in hbm else a for i, a in enumerate(args)])


def shape(*dims):
    return jax.ShapeDtypeStruct(dims, F32)


def elements(table, near, far, connect, shear, bulk, k_shear, k_bulk):
    rows = table.shape[0] + near.shape[0] + far.shape[0]
    elems = connect.shape[1]
    return call(
        element_kernel,
        [shape(table.shape[0], LO), shape(*near.shape), shape(*far.shape)],
        table,
        near,
        far,
        connect,
        shear,
        bulk,
        k_shear,
        k_bulk,
        scratch=[
            pltpu.VMEM((rows, 2 * LO), BF16),
            pltpu.VMEM((64, elems), F32),
            pltpu.VMEM((64, 64), F32),
            pltpu.VMEM((20, LO, elems), BF16),
            pltpu.VMEM((rows, LO), F32),
        ],
        flops=ELEMENT_FLOPS,
    )


def pack(displacement, seg_slave, dual, mortar, seg_face, seg_part, seg_count, n_dom):
    own = displacement.shape[1] // LO
    segs = seg_face.shape[0]
    return call(
        pack_kernel,
        [
            shape(n_dom, 1, 8 * WORDS),
            jax.ShapeDtypeStruct((2, segs), jnp.int32),
            jax.ShapeDtypeStruct((3 * own, 2 * LO), BF16),
            shape(3 * GHOST // LO, LO),
            shape(3 * GHOST // LO, LO),
        ],
        displacement,
        seg_slave,
        dual,
        mortar,
        seg_face[None],
        seg_part.reshape(1, segs),
        seg_count.reshape(1, 1),
        smem=(6,),
        hbm=(0, 1, 2, 3, 4, 5),
        scratch=[
            pltpu.VMEM((3 * own, LO), F32),
            pltpu.VMEM(displacement.shape, F32),
            pltpu.VMEM(seg_slave.shape, jnp.int32),
            pltpu.VMEM(dual.shape, F32),
            pltpu.VMEM(mortar.shape, F32),
            pltpu.VMEM((1, segs), jnp.int32),
            pltpu.VMEM((1, segs), jnp.int32),
            pltpu.SemaphoreType.DMA((6,)),
        ],
    )


def master(incoming, table, face_nodes):
    width = incoming.shape[0] * 8
    return call(
        master_kernel,
        [
            shape(width // 8, 1, 256),
            shape(24, width),
            jax.ShapeDtypeStruct((8, width), jnp.int32),
        ],
        incoming,
        table,
        face_nodes,
    )


def slave_side(returned, slot, dual, seg_slave, owned, master_part, near, far, n_sub):
    own = owned.shape[0] // 3
    return call(
        slave_kernel,
        shape(n_sub, 3 * own // n_sub, LO),
        returned,
        slot,
        dual,
        seg_slave,
        owned,
        master_part,
        near,
        far,
    )


def on_device(
    displacement,
    connect,
    shear,
    bulk,
    stiff_shear,
    stiff_bulk,
    seg_slave,
    seg_part,
    seg_face,
    face_nodes,
    dual,
    mortar,
    seg_count,
):
    nodes = displacement.shape[1]
    n_dom, n_sub = lax.axis_size("dom"), lax.axis_size("sub")
    group = sorted(range(n_dom), key=lambda part: place_in_group(part, n_dom))
    near_pairs = [(i, i ^ 1) for i in range(n_dom)]
    far_pairs = [(i, min(max(((i + 1) ^ 1) - 1, 0), n_dom - 1)) for i in range(n_dom)]
    outgoing, slot, table, near, far = pack(
        displacement, seg_slave, dual, mortar, seg_face, seg_part, seg_count, n_dom
    )
    incoming = lax.all_to_all(outgoing, "dom", 0, 0, axis_index_groups=[group], tiled=True)
    near = lax.ppermute(near, "dom", near_pairs)
    far = lax.ppermute(far, "dom", far_pairs)
    owned, near, far = elements(
        table, near, far, connect, shear, bulk, stiff_shear, stiff_bulk
    )
    incoming, owned = lax.optimization_barrier((incoming, owned))
    mult, master_force, master_nodes = master(incoming, table, face_nodes)
    returned = lax.all_to_all(mult, "dom", 0, 0, axis_index_groups=[group], tiled=True)
    near = lax.ppermute(near, "dom", near_pairs)
    far = lax.ppermute(far, "dom", far_pairs)
    master_part = call(
        master_scatter_kernel, shape(3 * nodes // LO, LO), master_force, master_nodes
    )
    blocks = slave_side(
        returned, slot, dual, seg_slave, owned, master_part, near, far, n_sub
    )
    me = lax.axis_index("sub")
    sent = [
        lax.ppermute(
            lax.dynamic_index_in_dim(blocks, (me + k) % n_sub, 0, keepdims=False),
            "sub",
            [(s, (s + k) % n_sub) for s in range(n_sub)],
        )
        for k in range(1, n_sub)
    ]
    mine = lax.dynamic_index_in_dim(blocks, me, 0, keepdims=False)
    return call(finish_kernel, shape(3, nodes // n_sub), mine, *sent)


def solution(mesh):
    placed = (
        P(None, "dom"),
        P(None, ("dom", "sub")),
        P(("dom", "sub")),
        P(("dom", "sub")),
        P(),
        P(),
        P(None, ("dom", "sub")),
        P(("dom", "sub"), None),
        P(("dom", "sub")),
        P(None, "dom"),
        P(None, ("dom", "sub")),
        P(None, ("dom", "sub")),
        P(("dom", "sub")),
    )
    return jax.shard_map(
        on_device, mesh=mesh, in_specs=placed, out_specs=P(None, ("dom", "sub")), check_vma=False
    )
```

```python
import jax
import jax.numpy as jnp
from jax import lax
from jax.experimental import pallas as pl
from jax.experimental.pallas import tpu as pltpu
from jax.sharding import PartitionSpec as P

GHOST = 2048
LO = 256
penalty = 2.0
WORDS = 96
ELEMENT_FLOPS = 8 * 10**9
F32 = jnp.float32
BF16 = jnp.bfloat16


def pieces(x):
    first = x.astype(BF16)
    second = (x - first.astype(F32)).astype(BF16)
    return first, second


def one_hot_lo(index):
    n = index.shape[1]
    rows = lax.broadcasted_iota(jnp.int16, (LO, n), 0)
    low = (index & (LO - 1)).astype(jnp.int16)
    return jnp.where(rows == low, jnp.bfloat16(1), jnp.bfloat16(0))


def hi_mask(index, rows):
    n = index.shape[1]
    return lax.broadcasted_iota(jnp.int32, (rows, n), 0) == (index >> 8)


def to_rows(source, offset, count, target, first_row, stride):
    for c in range(3):
        for h in range(count):
            row = c * stride + first_row + h
            target[row : row + 1, :] = source[c : c + 1, offset + h * LO : offset + (h + 1) * LO]


def gather_column(table, hot, mask):
    rows = mask.shape[0]
    picked = jnp.dot(table, jnp.concatenate([hot, hot], axis=0), preferred_element_type=F32)
    return [
        jnp.sum(jnp.where(mask, picked[c * rows : (c + 1) * rows], 0.0), axis=0, keepdims=True)
        for c in range(3)
    ]


def scatter_column(values, hot, mask):
    firsts, seconds = [], []
    for c in range(3):
        first, second = pieces(values[c])
        firsts.append(jnp.where(mask, first.astype(F32), 0.0).astype(BF16))
        seconds.append(jnp.where(mask, second.astype(F32), 0.0).astype(BF16))
    spread = jnp.concatenate(
        [jnp.concatenate(firsts, axis=0), jnp.concatenate(seconds, axis=0)], axis=1
    )
    return lax.dot_general(
        spread,
        jnp.concatenate([hot, hot], axis=1),
        (((1,), (1,)), ((), ())),
        preferred_element_type=F32,
    )


def gather(table, index, rows):
    return gather_column(table, one_hot_lo(index), hi_mask(index, rows))


def scatter(values, index, rows):
    return scatter_column(values, one_hot_lo(index), hi_mask(index, rows))


def by_side(near, far):
    here_dom, n_dom = lax.axis_index("dom"), lax.axis_size("dom")
    even = here_dom % 2 == 0
    below = jnp.where(here_dom == 0, 0.0, jnp.where(even, far, near))
    above = jnp.where(here_dom == n_dom - 1, 0.0, jnp.where(even, near, far))
    return below, above


def element_kernel(
    own, far, near, connect, shear, bulk, k_shear, k_bulk,
    owned, far_out, near_out, table, dofs, k_pad, hots, total,
):
    ghost = near.shape[0] // 3
    count = own.shape[0] // 3
    rows = count + 2 * ghost
    elems = connect.shape[1]
    for source, first_row in zip(by_side(near[...], far[...]), (0, rows - ghost)):
        first, second = pieces(source)
        for c in range(3):
            here = slice(c * rows + first_row, c * rows + first_row + ghost)
            table[here, :LO] = first[c * ghost : (c + 1) * ghost]
            table[here, LO:] = second[c * ghost : (c + 1) * ghost]
    for c in range(3):
        table[c * rows + ghost : c * rows + ghost + count, :] = own[c * count : (c + 1) * count, :]
    dofs[...] = jnp.zeros_like(dofs)
    for a in range(20):
        index = connect[a : a + 1, :]
        hot = one_hot_lo(index)
        hots[a] = hot
        got = gather_column(table[...], hot, hi_mask(index, rows))
        for c in range(3):
            dofs[20 * c + a : 20 * c + a + 1, :] = got[c]
    g_first, g_second = pieces(dofs[...])
    g = jnp.concatenate([g_first, g_first, g_second, g_second], axis=0)

    def product(k):
        k_pad[...] = jnp.zeros_like(k_pad)
        k_pad[: k.shape[0], : k.shape[1]] = k[...]
        k_first, k_second = pieces(k_pad[...].T)
        wide = jnp.concatenate([k_first, k_second, k_first, k_second], axis=1)
        return jnp.dot(wide, g, preferred_element_type=F32)

    by_shear, by_bulk = (m[...].reshape(1, elems) for m in (shear, bulk))
    dofs[...] = by_shear * product(k_shear) + by_bulk * product(k_bulk)
    total[...] = jnp.zeros_like(total)
    for a in range(20):
        values = [dofs[20 * c + a : 20 * c + a + 1, :] for c in range(3)]
        total[...] += scatter_column(values, hots[a], hi_mask(connect[a : a + 1, :], rows))
    even = lax.axis_index("dom") % 2 == 0
    for c in range(3):
        base = c * rows
        here = slice(c * ghost, (c + 1) * ghost)
        low = total[base : base + ghost, :]
        high = total[base + ghost + count : base + rows, :]
        near_out[here, :] = jnp.where(even, high, low)
        far_out[here, :] = jnp.where(even, low, high)
        owned[c * count : (c + 1) * count, :] = total[base + ghost : base + ghost + count, :]


def place_in_group(part, n_dom):
    ny, nz = 4, n_dom // 8
    y, z, core = part // (2 * nz), (part // 2) % nz, part % 2
    return n_dom - 1 - (z * (2 * ny) + y * 2 + core)


def pack_kernel(*refs):
    given, (count, out, slot_out, table, far, near, rows) = refs[:6], refs[6:13]
    held, sems = refs[13:19], refs[19]
    copies = [pltpu.make_async_copy(a, b, sems.at[i]) for i, (a, b) in enumerate(zip(given, held))]
    for copy in copies:
        copy.start()
    for copy in copies:
        copy.wait()
    disp, slave, dual, mortar, face, part = held
    segs = slave.shape[1]
    own = disp.shape[1] // LO
    to_rows(disp, 0, own, rows, 0, own)
    first, second = pieces(rows[...])
    packed = jnp.concatenate([first, second], axis=1)
    table[...] = packed
    ghost = GHOST // LO
    even = lax.axis_index("dom") % 2 == 0
    for c in range(3):
        head = rows[c * own : c * own + ghost, :]
        tail = rows[(c + 1) * own - ghost : (c + 1) * own, :]
        near[c * ghost : (c + 1) * ghost, :] = jnp.where(even, tail, head)
        far[c * ghost : (c + 1) * ghost, :] = jnp.where(even, head, tail)
    cap = 8
    n_dom = out.shape[0]
    width = n_dom * cap
    lanes = lax.broadcasted_iota(jnp.int32, (1, segs), 1)
    live = jnp.where(lanes < count[0, 0], 1.0, 0.0)
    vals = []
    for i in range(8):
        vals.append(gather(packed, slave[i : i + 1, :], own))
    slave_part = [
        (dual[i : i + 1, :] * live) * vals[i][c] for c in range(3) for i in range(8)
    ]
    payload = jnp.concatenate(
        slave_part
        + [mortar[...] * live, face[...].astype(F32), jnp.zeros((WORDS - 89, segs), F32)],
        axis=0,
    )
    hits = lax.broadcasted_iota(jnp.int32, (n_dom, segs), 0) == part[...]
    hits_b = jnp.where(hits, 1.0, 0.0).astype(BF16)
    earlier = (
        lax.broadcasted_iota(jnp.int32, (segs, segs), 0)
        < lax.broadcasted_iota(jnp.int32, (segs, segs), 1)
    )
    before = jnp.dot(
        hits_b, jnp.where(earlier, 1.0, 0.0).astype(BF16), preferred_element_type=F32
    )
    rank = jnp.sum(jnp.where(hits, before, 0.0), axis=0, keepdims=True).astype(jnp.int32)
    place_of = place_in_group(part[...], n_dom)
    slot = rank * n_dom + place_of
    slot_out[0:1, :] = place_of
    slot_out[1:2, :] = rank
    place = jnp.where(
        lax.broadcasted_iota(jnp.int32, (width, segs), 0) == slot, 1.0, 0.0
    ).astype(BF16)
    p1 = payload.astype(BF16)
    rest = payload - p1.astype(F32)
    p2 = rest.astype(BF16)
    placed = lax.dot_general(
        jnp.concatenate([place, place], axis=1),
        jnp.concatenate([p1, p2], axis=1),
        (((1,), (1,)), ((), ())),
        preferred_element_type=F32,
    )
    for k in range(cap):
        out[:, 0, WORDS * k : WORDS * (k + 1)] = placed[n_dom * k : n_dom * (k + 1), :]


def master_kernel(incoming, table, faces, mult_out, force_out, nodes_out):
    own = table.shape[0] // 3
    n_dom = incoming.shape[0]
    width = n_dom * 8
    packed = table[...]
    got = jnp.concatenate(
        [incoming[:, 0, WORDS * k : WORDS * (k + 1)] for k in range(8)], axis=0
    ).T
    face = got[88:89, :].astype(jnp.int32)
    groups = faces.shape[1] // LO
    listing = jnp.concatenate([faces[:, g * LO : (g + 1) * LO] for g in range(groups)], axis=0)
    f_first = (listing >> 7).astype(F32).astype(BF16)
    f_second = (listing & 127).astype(F32).astype(BF16)
    hot = one_hot_lo(face)
    f_table = jnp.concatenate([f_first, f_second], axis=0)
    picked = jnp.dot(f_table, hot, preferred_element_type=F32)
    both = picked[: 8 * groups] * 128.0 + picked[8 * groups :]
    face_hi = face >> 8
    nodes = jnp.zeros((8, width), F32)
    for g in range(groups):
        nodes = nodes + jnp.where(face_hi == g, both[8 * g : 8 * (g + 1)], 0.0)
    nodes = nodes.astype(jnp.int32)
    nodes_out[...] = nodes
    vals = [gather(packed, nodes[j : j + 1, :], own) for j in range(8)]
    matrix = [got[24 + 8 * i : 32 + 8 * i, :] for i in range(8)]
    mults = []
    for c in range(3):
        master = jnp.concatenate([vals[j][c] for j in range(8)], axis=0)
        force = jnp.zeros((8, width), F32)
        for i in range(8):
            gap = got[8 * c + i : 8 * c + i + 1, :] - jnp.sum(
                matrix[i] * master, axis=0, keepdims=True
            )
            mult = penalty * gap
            mults.append(mult)
            force = force - matrix[i] * mult
        force_out[8 * c : 8 * c + 8, :] = force
    back = jnp.concatenate(mults + [jnp.zeros((8, width), F32)], axis=0).T
    for k in range(8):
        mult_out[:, 0, 32 * k : 32 * (k + 1)] = back[n_dom * k : n_dom * (k + 1), :]


def master_scatter_kernel(force, nodes, out):
    own = out.shape[0] // 3
    total = jnp.zeros(out.shape, F32)
    for j in range(8):
        values = [force[8 * c + j : 8 * c + j + 1, :] for c in range(3)]
        total = total + scatter(values, nodes[j : j + 1, :], own)
    out[...] = total


def slave_kernel(returned, slot, dual, slave, owned, master, far, near, out):
    lower, upper = by_side(near[...], far[...])
    own = owned.shape[0] // 3
    ghost = near.shape[0] // 3
    segs = slot.shape[1]
    n_dom = returned.shape[0]
    mult_rows = returned[...].reshape(n_dom, 256).T
    m1 = mult_rows.astype(BF16)
    rest = mult_rows - m1.astype(F32)
    m2 = rest.astype(BF16)
    hot = jnp.where(
        lax.broadcasted_iota(jnp.int32, (n_dom, segs), 0) == slot[0:1, :], 1.0, 0.0
    ).astype(BF16)
    picked = jnp.dot(
        jnp.concatenate([m1, m2], axis=1),
        jnp.concatenate([hot, hot], axis=0),
        preferred_element_type=F32,
    )
    rank = slot[1:2, :]
    mult = jnp.zeros((32, segs), F32)
    for k in range(8):
        mult = mult + jnp.where(rank == k, picked[32 * k : 32 * (k + 1)], 0.0)
    total = owned[...] + master[...]
    for i in range(8):
        values = [dual[i : i + 1, :] * mult[8 * c + i : 8 * c + i + 1, :] for c in range(3)]
        total = total + scatter(values, slave[i : i + 1, :], own)
    quarters = out.shape[0]
    per = own // quarters
    for c in range(3):
        block = total[c * own : (c + 1) * own]
        for q in range(quarters):
            part = block[q * per : (q + 1) * per]
            if q == 0:
                part = jnp.concatenate(
                    [part[:ghost] + lower[c * ghost : (c + 1) * ghost], part[ghost:]], axis=0
                )
            if q == quarters - 1:
                part = jnp.concatenate(
                    [part[:-ghost], part[-ghost:] + upper[c * ghost : (c + 1) * ghost]], axis=0
                )
            out[q, c * per : (c + 1) * per, :] = part


def finish_kernel(own_part, a, b, d, out):
    per = own_part.shape[0] // 3
    total = own_part[...] + a[...] + b[...] + d[...]
    for c in range(3):
        for h in range(per):
            out[c : c + 1, h * LO : (h + 1) * LO] = total[c * per + h : c * per + h + 1, :]


def call(kernel, outs, *args, scratch=(), smem=(), hbm=(), flops=10**8):
    specs = [
        pl.BlockSpec(
            memory_space=pltpu.SMEM if i in smem else pltpu.HBM if i in hbm else pltpu.VMEM
        )
        for i in range(len(args))
    ]
    moved = sum(a.size * 4 for a in args)
    many = isinstance(outs, list)
    return pl.pallas_call(
        kernel,
        out_shape=outs,
        in_specs=specs,
        out_specs=[pl.BlockSpec(memory_space=pltpu.VMEM)] * len(outs)
        if many
        else pl.BlockSpec(memory_space=pltpu.VMEM),
        scratch_shapes=list(scratch),
        cost_estimate=pl.CostEstimate(flops=flops, transcendentals=0, bytes_accessed=moved),
        compiler_params=pltpu.CompilerParams(vmem_limit_bytes=48 * 1024 * 1024),
    )(*[pltpu.with_memory_space_constraint(a, pltpu.HBM) if i in hbm else a for i, a in enumerate(args)])


def shape(*dims):
    return jax.ShapeDtypeStruct(dims, F32)


def elements(table, near, far, connect, shear, bulk, k_shear, k_bulk):
    rows = table.shape[0] + near.shape[0] + far.shape[0]
    elems = connect.shape[1]
    return call(
        element_kernel,
        [shape(table.shape[0], LO), shape(*near.shape), shape(*far.shape)],
        table,
        far,
        near,
        connect,
        shear,
        bulk,
        k_shear,
        k_bulk,
        scratch=[
            pltpu.VMEM((rows, 2 * LO), BF16),
            pltpu.VMEM((64, elems), F32),
            pltpu.VMEM((64, 64), F32),
            pltpu.VMEM((20, LO, elems), BF16),
            pltpu.VMEM((rows, LO), F32),
        ],
        flops=ELEMENT_FLOPS,
    )


def pack(displacement, seg_slave, dual, mortar, seg_face, seg_part, seg_count, n_dom):
    own = displacement.shape[1] // LO
    segs = seg_face.shape[0]
    return call(
        pack_kernel,
        [
            shape(n_dom, 1, 8 * WORDS),
            jax.ShapeDtypeStruct((2, segs), jnp.int32),
            jax.ShapeDtypeStruct((3 * own, 2 * LO), BF16),
            shape(3 * GHOST // LO, LO),
            shape(3 * GHOST // LO, LO),
        ],
        displacement,
        seg_slave,
        dual,
        mortar,
        seg_face[None],
        seg_part.reshape(1, segs),
        seg_count.reshape(1, 1),
        smem=(6,),
        hbm=(0, 1, 2, 3, 4, 5),
        scratch=[
            pltpu.VMEM((3 * own, LO), F32),
            pltpu.VMEM(displacement.shape, F32),
            pltpu.VMEM(seg_slave.shape, jnp.int32),
            pltpu.VMEM(dual.shape, F32),
            pltpu.VMEM(mortar.shape, F32),
            pltpu.VMEM((1, segs), jnp.int32),
            pltpu.VMEM((1, segs), jnp.int32),
            pltpu.SemaphoreType.DMA((6,)),
        ],
    )


def master(incoming, table, face_nodes):
    width = incoming.shape[0] * 8
    return call(
        master_kernel,
        [
            shape(width // 8, 1, 256),
            shape(24, width),
            jax.ShapeDtypeStruct((8, width), jnp.int32),
        ],
        incoming,
        table,
        face_nodes,
    )


def slave_side(returned, slot, dual, seg_slave, owned, master_part, near, far, n_sub):
    own = owned.shape[0] // 3
    return call(
        slave_kernel,
        shape(n_sub, 3 * own // n_sub, LO),
        returned,
        slot,
        dual,
        seg_slave,
        owned,
        master_part,
        far,
        near,
    )


def on_device(
    displacement,
    connect,
    shear,
    bulk,
    stiff_shear,
    stiff_bulk,
    seg_slave,
    seg_part,
    seg_face,
    face_nodes,
    dual,
    mortar,
    seg_count,
):
    nodes = displacement.shape[1]
    n_dom, n_sub = lax.axis_size("dom"), lax.axis_size("sub")
    group = sorted(range(n_dom), key=lambda part: place_in_group(part, n_dom))
    near_pairs = [(i, i ^ 1) for i in range(n_dom)]
    far_pairs = [(i, min(max(((i + 1) ^ 1) - 1, 0), n_dom - 1)) for i in range(n_dom)]
    outgoing, slot, table, far, near = pack(
        displacement, seg_slave, dual, mortar, seg_face, seg_part, seg_count, n_dom
    )
    incoming = lax.all_to_all(outgoing, "dom", 0, 0, axis_index_groups=[group], tiled=True)
    far = lax.ppermute(far, "dom", far_pairs)
    near = lax.ppermute(near, "dom", near_pairs)
    owned, far, near = elements(
        table, near, far, connect, shear, bulk, stiff_shear, stiff_bulk
    )
    incoming, owned = lax.optimization_barrier((incoming, owned))
    mult, master_force, master_nodes = master(incoming, table, face_nodes)
    returned = lax.all_to_all(mult, "dom", 0, 0, axis_index_groups=[group], tiled=True)
    far = lax.ppermute(far, "dom", far_pairs)
    near = lax.ppermute(near, "dom", near_pairs)
    master_part = call(
        master_scatter_kernel, shape(3 * nodes // LO, LO), master_force, master_nodes
    )
    blocks = slave_side(
        returned, slot, dual, seg_slave, owned, master_part, near, far, n_sub
    )
    me = lax.axis_index("sub")
    sent = [
        lax.ppermute(
            lax.dynamic_index_in_dim(blocks, (me + k) % n_sub, 0, keepdims=False),
            "sub",
            [(s, (s + k) % n_sub) for s in range(n_sub)],
        )
        for k in range(1, n_sub)
    ]
    mine = lax.dynamic_index_in_dim(blocks, me, 0, keepdims=False)
    return call(finish_kernel, shape(3, nodes // n_sub), mine, *sent)


def solution(mesh):
    placed = (
        P(None, "dom"),
        P(None, ("dom", "sub")),
        P(("dom", "sub")),
        P(("dom", "sub")),
        P(),
        P(),
        P(None, ("dom", "sub")),
        P(("dom", "sub"), None),
        P(("dom", "sub")),
        P(None, "dom"),
        P(None, ("dom", "sub")),
        P(None, ("dom", "sub")),
        P(("dom", "sub")),
    )
    return jax.shard_map(
        on_device, mesh=mesh, in_specs=placed, out_specs=P(None, ("dom", "sub")), check_vma=False
    )
```

```python
import jax
import jax.numpy as jnp
from jax import lax
from jax.experimental import pallas as pl
from jax.experimental.pallas import tpu as pltpu
from jax.sharding import PartitionSpec as P

GHOST = 2048
LO = 256
penalty = 2.0
ELEMENT_FLOPS = 8 * 10**9
F32 = jnp.float32
BF16 = jnp.bfloat16


def pieces(x):
    first = x.astype(BF16)
    second = (x - first.astype(F32)).astype(BF16)
    return first, second


def one_hot_lo(index):
    n = index.shape[1]
    rows = lax.broadcasted_iota(jnp.int16, (LO, n), 0)
    low = (index & (LO - 1)).astype(jnp.int16)
    return jnp.where(rows == low, jnp.bfloat16(1), jnp.bfloat16(0))


def hi_mask(index, rows):
    n = index.shape[1]
    return lax.broadcasted_iota(jnp.int32, (rows, n), 0) == (index >> 8)


def to_rows(source, offset, count, target, first_row, stride):
    for c in range(3):
        for h in range(count):
            row = c * stride + first_row + h
            target[row : row + 1, :] = source[c : c + 1, offset + h * LO : offset + (h + 1) * LO]


def gather_column(table, hot, mask):
    rows = mask.shape[0]
    picked = jnp.dot(table, jnp.concatenate([hot, hot], axis=0), preferred_element_type=F32)
    return [
        jnp.sum(jnp.where(mask, picked[c * rows : (c + 1) * rows], 0.0), axis=0, keepdims=True)
        for c in range(3)
    ]


def scatter_column(values, hot, mask):
    firsts, seconds = [], []
    for c in range(3):
        first, second = pieces(values[c])
        firsts.append(jnp.where(mask, first.astype(F32), 0.0).astype(BF16))
        seconds.append(jnp.where(mask, second.astype(F32), 0.0).astype(BF16))
    spread = jnp.concatenate(
        [jnp.concatenate(firsts, axis=0), jnp.concatenate(seconds, axis=0)], axis=1
    )
    return lax.dot_general(
        spread,
        jnp.concatenate([hot, hot], axis=1),
        (((1,), (1,)), ((), ())),
        preferred_element_type=F32,
    )


def gather(table, index, rows):
    return gather_column(table, one_hot_lo(index), hi_mask(index, rows))


def scatter(values, index, rows):
    return scatter_column(values, one_hot_lo(index), hi_mask(index, rows))


def by_side(near, far):
    here_dom, n_dom = lax.axis_index("dom"), lax.axis_size("dom")
    even = here_dom % 2 == 0
    below = jnp.where(here_dom == 0, 0.0, jnp.where(even, far, near))
    above = jnp.where(here_dom == n_dom - 1, 0.0, jnp.where(even, near, far))
    return below, above


def element_kernel(
    own, near, far, connect, shear, bulk, k_shear, k_bulk,
    owned, near_out, far_out, table, dofs, k_pad, hots, total,
):
    ghost = near.shape[0] // 3
    count = own.shape[0] // 3
    rows = count + 2 * ghost
    elems = connect.shape[1]
    for source, first_row in zip(by_side(near[...], far[...]), (0, rows - ghost)):
        first, second = pieces(source)
        for c in range(3):
            here = slice(c * rows + first_row, c * rows + first_row + ghost)
            table[here, :LO] = first[c * ghost : (c + 1) * ghost]
            table[here, LO:] = second[c * ghost : (c + 1) * ghost]
    for c in range(3):
        table[c * rows + ghost : c * rows + ghost + count, :] = own[c * count : (c + 1) * count, :]
    dofs[...] = jnp.zeros_like(dofs)
    for a in range(20):
        index = connect[a : a + 1, :]
        hot = one_hot_lo(index)
        hots[a] = hot
        got = gather_column(table[...], hot, hi_mask(index, rows))
        for c in range(3):
            dofs[20 * c + a : 20 * c + a + 1, :] = got[c]
    g_first, g_second = pieces(dofs[...])
    g = jnp.concatenate([g_first, g_first, g_second, g_second], axis=0)

    def product(k):
        k_pad[...] = jnp.zeros_like(k_pad)
        k_pad[: k.shape[0], : k.shape[1]] = k[...]
        k_first, k_second = pieces(k_pad[...].T)
        wide = jnp.concatenate([k_first, k_second, k_first, k_second], axis=1)
        return jnp.dot(wide, g, preferred_element_type=F32)

    by_shear, by_bulk = (m[...].reshape(1, elems) for m in (shear, bulk))
    dofs[...] = by_shear * product(k_shear) + by_bulk * product(k_bulk)
    total[...] = jnp.zeros_like(total)
    for a in range(20):
        values = [dofs[20 * c + a : 20 * c + a + 1, :] for c in range(3)]
        total[...] += scatter_column(values, hots[a], hi_mask(connect[a : a + 1, :], rows))
    even = lax.axis_index("dom") % 2 == 0
    for c in range(3):
        base = c * rows
        here = slice(c * ghost, (c + 1) * ghost)
        low = total[base : base + ghost, :]
        high = total[base + ghost + count : base + rows, :]
        near_out[here, :] = jnp.where(even, high, low)
        far_out[here, :] = jnp.where(even, low, high)
        owned[c * count : (c + 1) * count, :] = total[base + ghost : base + ghost + count, :]


def place_in_group(part, n_dom):
    ny, nz = 4, n_dom // 8
    y, z, core = part // (2 * nz), (part // 2) % nz, part % 2
    return n_dom - 1 - (z * (2 * ny) + y * 2 + core)


def pack_kernel(*refs):
    given, (count, out, slot_out, table, near, far, rows) = refs[:6], refs[6:13]
    held, sems = refs[13:19], refs[19]
    copies = [pltpu.make_async_copy(a, b, sems.at[i]) for i, (a, b) in enumerate(zip(given, held))]
    for copy in copies:
        copy.start()
    for copy in copies:
        copy.wait()
    disp, slave, dual, mortar, face, part = held
    segs = slave.shape[1]
    own = disp.shape[1] // LO
    to_rows(disp, 0, own, rows, 0, own)
    first, second = pieces(rows[...])
    packed = jnp.concatenate([first, second], axis=1)
    table[...] = packed
    ghost = GHOST // LO
    even = lax.axis_index("dom") % 2 == 0
    for c in range(3):
        head = rows[c * own : c * own + ghost, :]
        tail = rows[(c + 1) * own - ghost : (c + 1) * own, :]
        near[c * ghost : (c + 1) * ghost, :] = jnp.where(even, tail, head)
        far[c * ghost : (c + 1) * ghost, :] = jnp.where(even, head, tail)
    cap = 8
    width = out.shape[0]
    n_dom = width // cap
    lanes = lax.broadcasted_iota(jnp.int32, (1, segs), 1)
    live = jnp.where(lanes < count[0, 0], 1.0, 0.0)
    vals = []
    for i in range(8):
        vals.append(gather(packed, slave[i : i + 1, :], own))
    slave_part = [
        (dual[i : i + 1, :] * live) * vals[i][c] for c in range(3) for i in range(8)
    ]
    payload = jnp.concatenate(
        slave_part
        + [mortar[...] * live, face[...].astype(F32), jnp.zeros((39, segs), F32)],
        axis=0,
    )
    hits = lax.broadcasted_iota(jnp.int32, (n_dom, segs), 0) == part[...]
    hits_b = jnp.where(hits, 1.0, 0.0).astype(BF16)
    earlier = (
        lax.broadcasted_iota(jnp.int32, (segs, segs), 0)
        < lax.broadcasted_iota(jnp.int32, (segs, segs), 1)
    )
    before = jnp.dot(
        hits_b, jnp.where(earlier, 1.0, 0.0).astype(BF16), preferred_element_type=F32
    )
    rank = jnp.sum(jnp.where(hits, before, 0.0), axis=0, keepdims=True).astype(jnp.int32)
    slot = place_in_group(part[...], n_dom) * cap + rank
    slot_out[...] = slot
    place = jnp.where(
        lax.broadcasted_iota(jnp.int32, (width, segs), 0) == slot, 1.0, 0.0
    ).astype(BF16)
    p1 = payload.astype(BF16)
    rest = payload - p1.astype(F32)
    p2 = rest.astype(BF16)
    p3 = (rest - p2.astype(F32)).astype(BF16)
    out[...] = lax.dot_general(
        jnp.concatenate([place, place, place], axis=1),
        jnp.concatenate([p1, p2, p3], axis=1),
        (((1,), (1,)), ((), ())),
        preferred_element_type=F32,
    )


def master_kernel(incoming, table, faces, mult_out, force_out, nodes_out):
    own = table.shape[0] // 3
    width = incoming.shape[0]
    n_dom = width // 8
    packed = table[...]
    got = incoming[...].T
    face = got[88:89, :].astype(jnp.int32)
    groups = faces.shape[1] // LO
    listing = jnp.concatenate([faces[:, g * LO : (g + 1) * LO] for g in range(groups)], axis=0)
    f_first = (listing >> 7).astype(F32).astype(BF16)
    f_second = (listing & 127).astype(F32).astype(BF16)
    hot = one_hot_lo(face)
    f_table = jnp.concatenate([f_first, f_second], axis=0)
    picked = jnp.dot(f_table, hot, preferred_element_type=F32)
    both = picked[: 8 * groups] * 128.0 + picked[8 * groups :]
    face_hi = face >> 8
    nodes = jnp.zeros((8, width), F32)
    for g in range(groups):
        nodes = nodes + jnp.where(face_hi == g, both[8 * g : 8 * (g + 1)], 0.0)
    nodes = nodes.astype(jnp.int32)
    nodes_out[...] = nodes
    vals = [gather(packed, nodes[j : j + 1, :], own) for j in range(8)]
    matrix = [got[24 + 8 * i : 32 + 8 * i, :] for i in range(8)]
    mults = []
    for c in range(3):
        master = jnp.concatenate([vals[j][c] for j in range(8)], axis=0)
        force = jnp.zeros((8, width), F32)
        for i in range(8):
            gap = got[8 * c + i : 8 * c + i + 1, :] - jnp.sum(
                matrix[i] * master, axis=0, keepdims=True
            )
            mult = penalty * gap
            mults.append(mult)
            force = force - matrix[i] * mult
        force_out[8 * c : 8 * c + 8, :] = force
    back = jnp.concatenate(mults + [jnp.zeros((8, width), F32)], axis=0).T
    back = back.reshape(n_dom, 8, 32)
    for k in range(8):
        mult_out[:, 0, 32 * k : 32 * (k + 1)] = back[:, k, :]


def master_scatter_kernel(force, nodes, out):
    own = out.shape[0] // 3
    total = jnp.zeros(out.shape, F32)
    for j in range(8):
        values = [force[8 * c + j : 8 * c + j + 1, :] for c in range(3)]
        total = total + scatter(values, nodes[j : j + 1, :], own)
    out[...] = total


def slave_kernel(returned, slot, dual, slave, owned, master, near, far, out):
    lower, upper = by_side(near[...], far[...])
    own = owned.shape[0] // 3
    ghost = near.shape[0] // 3
    segs = slot.shape[1]
    n_dom = returned.shape[0]
    mult_rows = returned[...].reshape(n_dom, 256).T
    m1 = mult_rows.astype(BF16)
    rest = mult_rows - m1.astype(F32)
    m2 = rest.astype(BF16)
    m3 = (rest - m2.astype(F32)).astype(BF16)
    hot = jnp.where(
        lax.broadcasted_iota(jnp.int32, (n_dom, segs), 0) == (slot[...] >> 3), 1.0, 0.0
    ).astype(BF16)
    picked = jnp.dot(
        jnp.concatenate([m1, m2, m3], axis=1),
        jnp.concatenate([hot, hot, hot], axis=0),
        preferred_element_type=F32,
    )
    rank = slot[...] & 7
    mult = jnp.zeros((32, segs), F32)
    for k in range(8):
        mult = mult + jnp.where(rank == k, picked[32 * k : 32 * (k + 1)], 0.0)
    total = owned[...] + master[...]
    for i in range(8):
        values = [dual[i : i + 1, :] * mult[8 * c + i : 8 * c + i + 1, :] for c in range(3)]
        total = total + scatter(values, slave[i : i + 1, :], own)
    quarters = out.shape[0]
    per = own // quarters
    for c in range(3):
        block = total[c * own : (c + 1) * own]
        for q in range(quarters):
            part = block[q * per : (q + 1) * per]
            if q == 0:
                part = jnp.concatenate(
                    [part[:ghost] + lower[c * ghost : (c + 1) * ghost], part[ghost:]], axis=0
                )
            if q == quarters - 1:
                part = jnp.concatenate(
                    [part[:-ghost], part[-ghost:] + upper[c * ghost : (c + 1) * ghost]], axis=0
                )
            out[q, c * per : (c + 1) * per, :] = part


def finish_kernel(own_part, a, b, d, out):
    per = own_part.shape[0] // 3
    total = own_part[...] + a[...] + b[...] + d[...]
    for c in range(3):
        for h in range(per):
            out[c : c + 1, h * LO : (h + 1) * LO] = total[c * per + h : c * per + h + 1, :]


def call(kernel, outs, *args, scratch=(), smem=(), hbm=(), flops=10**8):
    specs = [
        pl.BlockSpec(
            memory_space=pltpu.SMEM if i in smem else pltpu.HBM if i in hbm else pltpu.VMEM
        )
        for i in range(len(args))
    ]
    moved = sum(a.size * 4 for a in args)
    many = isinstance(outs, list)
    return pl.pallas_call(
        kernel,
        out_shape=outs,
        in_specs=specs,
        out_specs=[pl.BlockSpec(memory_space=pltpu.VMEM)] * len(outs)
        if many
        else pl.BlockSpec(memory_space=pltpu.VMEM),
        scratch_shapes=list(scratch),
        cost_estimate=pl.CostEstimate(flops=flops, transcendentals=0, bytes_accessed=moved),
        compiler_params=pltpu.CompilerParams(vmem_limit_bytes=48 * 1024 * 1024),
    )(*[pltpu.with_memory_space_constraint(a, pltpu.HBM) if i in hbm else a for i, a in enumerate(args)])


def shape(*dims):
    return jax.ShapeDtypeStruct(dims, F32)


def elements(table, near, far, connect, shear, bulk, k_shear, k_bulk):
    rows = table.shape[0] + near.shape[0] + far.shape[0]
    elems = connect.shape[1]
    return call(
        element_kernel,
        [shape(table.shape[0], LO), shape(*near.shape), shape(*far.shape)],
        table,
        near,
        far,
        connect,
        shear,
        bulk,
        k_shear,
        k_bulk,
        scratch=[
            pltpu.VMEM((rows, 2 * LO), BF16),
            pltpu.VMEM((64, elems), F32),
            pltpu.VMEM((64, 64), F32),
            pltpu.VMEM((20, LO, elems), BF16),
            pltpu.VMEM((rows, LO), F32),
        ],
        flops=ELEMENT_FLOPS,
    )


def pack(displacement, seg_slave, dual, mortar, seg_face, seg_part, seg_count, n_dom):
    own = displacement.shape[1] // LO
    segs = seg_face.shape[0]
    return call(
        pack_kernel,
        [
            shape(n_dom * 8, 128),
            jax.ShapeDtypeStruct((1, segs), jnp.int32),
            jax.ShapeDtypeStruct((3 * own, 2 * LO), BF16),
            shape(3 * GHOST // LO, LO),
            shape(3 * GHOST // LO, LO),
        ],
        displacement,
        seg_slave,
        dual,
        mortar,
        seg_face[None],
        seg_part.reshape(1, segs),
        seg_count.reshape(1, 1),
        smem=(6,),
        hbm=(0, 1, 2, 3, 4, 5),
        scratch=[
            pltpu.VMEM((3 * own, LO), F32),
            pltpu.VMEM(displacement.shape, F32),
            pltpu.VMEM(seg_slave.shape, jnp.int32),
            pltpu.VMEM(dual.shape, F32),
            pltpu.VMEM(mortar.shape, F32),
            pltpu.VMEM((1, segs), jnp.int32),
            pltpu.VMEM((1, segs), jnp.int32),
            pltpu.SemaphoreType.DMA((6,)),
        ],
    )


def master(incoming, table, face_nodes):
    width = incoming.shape[0]
    return call(
        master_kernel,
        [
            shape(width // 8, 1, 256),
            shape(24, width),
            jax.ShapeDtypeStruct((8, width), jnp.int32),
        ],
        incoming,
        table,
        face_nodes,
    )


def slave_side(returned, slot, dual, seg_slave, owned, master_part, near, far, n_sub):
    own = owned.shape[0] // 3
    return call(
        slave_kernel,
        shape(n_sub, 3 * own // n_sub, LO),
        returned,
        slot,
        dual,
        seg_slave,
        owned,
        master_part,
        near,
        far,
    )


def on_device(
    displacement,
    connect,
    shear,
    bulk,
    stiff_shear,
    stiff_bulk,
    seg_slave,
    seg_part,
    seg_face,
    face_nodes,
    dual,
    mortar,
    seg_count,
):
    nodes = displacement.shape[1]
    n_dom, n_sub = lax.axis_size("dom"), lax.axis_size("sub")
    group = sorted(range(n_dom), key=lambda part: place_in_group(part, n_dom))
    near_pairs = [(i, i ^ 1) for i in range(n_dom)]
    far_pairs = [(i, min(max(((i + 1) ^ 1) - 1, 0), n_dom - 1)) for i in range(n_dom)]
    outgoing, slot, table, near, far = pack(
        displacement, seg_slave, dual, mortar, seg_face, seg_part, seg_count, n_dom
    )
    incoming = lax.all_to_all(
        outgoing.reshape(n_dom, 8, 128), "dom", 0, 0, axis_index_groups=[group], tiled=True
    )
    near = lax.ppermute(near, "dom", near_pairs)
    far = lax.ppermute(far, "dom", far_pairs)
    owned, near, far = elements(
        table, near, far, connect, shear, bulk, stiff_shear, stiff_bulk
    )
    incoming, owned = lax.optimization_barrier((incoming, owned))
    mult, master_force, master_nodes = master(
        incoming.reshape(n_dom * 8, 128), table, face_nodes
    )
    returned = lax.all_to_all(mult, "dom", 0, 0, axis_index_groups=[group], tiled=True)
    near = lax.ppermute(near, "dom", near_pairs)
    far = lax.ppermute(far, "dom", far_pairs)
    master_part = call(
        master_scatter_kernel, shape(3 * nodes // LO, LO), master_force, master_nodes
    )
    blocks = slave_side(
        returned, slot, dual, seg_slave, owned, master_part, near, far, n_sub
    )
    me = lax.axis_index("sub")
    sent = [
        lax.ppermute(
            lax.dynamic_index_in_dim(blocks, (me + k) % n_sub, 0, keepdims=False),
            "sub",
            [(s, (s + k) % n_sub) for s in range(n_sub)],
        )
        for k in range(1, n_sub)
    ]
    mine = lax.dynamic_index_in_dim(blocks, me, 0, keepdims=False)
    return call(finish_kernel, shape(3, nodes // n_sub), mine, *sent)


def solution(mesh):
    placed = (
        P(None, "dom"),
        P(None, ("dom", "sub")),
        P(("dom", "sub")),
        P(("dom", "sub")),
        P(),
        P(),
        P(None, ("dom", "sub")),
        P(("dom", "sub"), None),
        P(("dom", "sub")),
        P(None, "dom"),
        P(None, ("dom", "sub")),
        P(None, ("dom", "sub")),
        P(("dom", "sub")),
    )
    return jax.shard_map(
        on_device, mesh=mesh, in_specs=placed, out_specs=P(None, ("dom", "sub")), check_vma=False
    )
```

```python
import jax
import jax.numpy as jnp
from jax import lax
from jax.experimental import pallas as pl
from jax.experimental.pallas import tpu as pltpu
from jax.sharding import PartitionSpec as P

GHOST = 2048
LO = 256
penalty = 2.0
ELEMENT_FLOPS = 8 * 10**9
F32 = jnp.float32
BF16 = jnp.bfloat16


def pieces(x):
    first = x.astype(BF16)
    second = (x - first.astype(F32)).astype(BF16)
    return first, second


def one_hot_lo(index):
    n = index.shape[1]
    rows = lax.broadcasted_iota(jnp.int16, (LO, n), 0)
    low = (index & (LO - 1)).astype(jnp.int16)
    return jnp.where(rows == low, jnp.bfloat16(1), jnp.bfloat16(0))


def hi_mask(index, rows):
    n = index.shape[1]
    return lax.broadcasted_iota(jnp.int32, (rows, n), 0) == (index >> 8)


def to_rows(source, offset, count, target, first_row, stride):
    for c in range(3):
        for h in range(count):
            row = c * stride + first_row + h
            target[row : row + 1, :] = source[c : c + 1, offset + h * LO : offset + (h + 1) * LO]


def gather_column(table, hot, mask):
    rows = mask.shape[0]
    picked = jnp.dot(table, jnp.concatenate([hot, hot], axis=0), preferred_element_type=F32)
    return [
        jnp.sum(jnp.where(mask, picked[c * rows : (c + 1) * rows], 0.0), axis=0, keepdims=True)
        for c in range(3)
    ]


def scatter_column(values, hot, mask):
    firsts, seconds = [], []
    for c in range(3):
        first, second = pieces(values[c])
        firsts.append(jnp.where(mask, first.astype(F32), 0.0).astype(BF16))
        seconds.append(jnp.where(mask, second.astype(F32), 0.0).astype(BF16))
    spread = jnp.concatenate(
        [jnp.concatenate(firsts, axis=0), jnp.concatenate(seconds, axis=0)], axis=1
    )
    return lax.dot_general(
        spread,
        jnp.concatenate([hot, hot], axis=1),
        (((1,), (1,)), ((), ())),
        preferred_element_type=F32,
    )


def gather(table, index, rows):
    return gather_column(table, one_hot_lo(index), hi_mask(index, rows))


def scatter(values, index, rows):
    return scatter_column(values, one_hot_lo(index), hi_mask(index, rows))


def by_side(near, far):
    here_dom, n_dom = lax.axis_index("dom"), lax.axis_size("dom")
    even = here_dom % 2 == 0
    below = jnp.where(here_dom == 0, 0.0, jnp.where(even, far, near))
    above = jnp.where(here_dom == n_dom - 1, 0.0, jnp.where(even, near, far))
    return below, above


def element_kernel(
    own, near, far, connect, shear, bulk, k_shear, k_bulk,
    owned, near_out, far_out, table, dofs, k_pad, hots, total,
):
    ghost = near.shape[0] // 3
    count = own.shape[0] // 3
    rows = count + 2 * ghost
    elems = connect.shape[1]
    for source, first_row in zip(by_side(near[...], far[...]), (0, rows - ghost)):
        first, second = pieces(source)
        for c in range(3):
            here = slice(c * rows + first_row, c * rows + first_row + ghost)
            table[here, :LO] = first[c * ghost : (c + 1) * ghost]
            table[here, LO:] = second[c * ghost : (c + 1) * ghost]
    for c in range(3):
        table[c * rows + ghost : c * rows + ghost + count, :] = own[c * count : (c + 1) * count, :]
    dofs[...] = jnp.zeros_like(dofs)
    for a in range(20):
        index = connect[a : a + 1, :]
        hot = one_hot_lo(index)
        hots[a] = hot
        got = gather_column(table[...], hot, hi_mask(index, rows))
        for c in range(3):
            dofs[20 * c + a : 20 * c + a + 1, :] = got[c]
    g_first, g_second = pieces(dofs[...])
    g = jnp.concatenate([g_first, g_first, g_second, g_second], axis=0)

    def product(k):
        k_pad[...] = jnp.zeros_like(k_pad)
        k_pad[: k.shape[0], : k.shape[1]] = k[...]
        k_first, k_second = pieces(k_pad[...].T)
        wide = jnp.concatenate([k_first, k_second, k_first, k_second], axis=1)
        return jnp.dot(wide, g, preferred_element_type=F32)

    by_shear, by_bulk = (m[...].reshape(1, elems) for m in (shear, bulk))
    dofs[...] = by_shear * product(k_shear) + by_bulk * product(k_bulk)
    total[...] = jnp.zeros_like(total)
    for a in range(20):
        values = [dofs[20 * c + a : 20 * c + a + 1, :] for c in range(3)]
        total[...] += scatter_column(values, hots[a], hi_mask(connect[a : a + 1, :], rows))
    even = lax.axis_index("dom") % 2 == 0
    for c in range(3):
        base = c * rows
        here = slice(c * ghost, (c + 1) * ghost)
        low = total[base : base + ghost, :]
        high = total[base + ghost + count : base + rows, :]
        near_out[here, :] = jnp.where(even, high, low)
        far_out[here, :] = jnp.where(even, low, high)
        owned[c * count : (c + 1) * count, :] = total[base + ghost : base + ghost + count, :]


def place_in_group(part, n_dom):
    ny, nz = 4, n_dom // 8
    y, z, core = part // (2 * nz), (part // 2) % nz, part % 2
    return n_dom - 1 - (z * (2 * ny) + y * 2 + core)


def pack_kernel(*refs):
    given, (count, out, slot_out, table, near, far, rows) = refs[:6], refs[6:13]
    held, sems = refs[13:19], refs[19]
    copies = [pltpu.make_async_copy(a, b, sems.at[i]) for i, (a, b) in enumerate(zip(given, held))]
    for copy in copies:
        copy.start()
    for copy in copies:
        copy.wait()
    disp, slave, dual, mortar, face, part = held
    segs = slave.shape[1]
    own = disp.shape[1] // LO
    to_rows(disp, 0, own, rows, 0, own)
    first, second = pieces(rows[...])
    packed = jnp.concatenate([first, second], axis=1)
    table[...] = packed
    ghost = GHOST // LO
    even = lax.axis_index("dom") % 2 == 0
    for c in range(3):
        head = rows[c * own : c * own + ghost, :]
        tail = rows[(c + 1) * own - ghost : (c + 1) * own, :]
        near[c * ghost : (c + 1) * ghost, :] = jnp.where(even, tail, head)
        far[c * ghost : (c + 1) * ghost, :] = jnp.where(even, head, tail)
    cap = 8
    width = out.shape[0]
    n_dom = width // cap
    lanes = lax.broadcasted_iota(jnp.int32, (1, segs), 1)
    live = jnp.where(lanes < count[0, 0], 1.0, 0.0)
    vals = []
    for i in range(8):
        vals.append(gather(packed, slave[i : i + 1, :], own))
    slave_part = [
        (dual[i : i + 1, :] * live) * vals[i][c] for c in range(3) for i in range(8)
    ]
    payload = jnp.concatenate(
        slave_part
        + [mortar[...] * live, face[...].astype(F32), jnp.zeros((39, segs), F32)],
        axis=0,
    )
    hits = lax.broadcasted_iota(jnp.int32, (n_dom, segs), 0) == part[...]
    hits_b = jnp.where(hits, 1.0, 0.0).astype(BF16)
    earlier = (
        lax.broadcasted_iota(jnp.int32, (segs, segs), 0)
        < lax.broadcasted_iota(jnp.int32, (segs, segs), 1)
    )
    before = jnp.dot(
        hits_b, jnp.where(earlier, 1.0, 0.0).astype(BF16), preferred_element_type=F32
    )
    rank = jnp.sum(jnp.where(hits, before, 0.0), axis=0, keepdims=True).astype(jnp.int32)
    slot = place_in_group(part[...], n_dom) * cap + rank
    slot_out[...] = slot
    place = jnp.where(
        lax.broadcasted_iota(jnp.int32, (width, segs), 0) == slot, 1.0, 0.0
    ).astype(BF16)
    p1 = payload.astype(BF16)
    rest = payload - p1.astype(F32)
    p2 = rest.astype(BF16)
    out[...] = lax.dot_general(
        jnp.concatenate([place, place], axis=1),
        jnp.concatenate([p1, p2], axis=1),
        (((1,), (1,)), ((), ())),
        preferred_element_type=F32,
    )


def master_kernel(incoming, table, faces, mult_out, force_out, nodes_out):
    own = table.shape[0] // 3
    width = incoming.shape[0]
    n_dom = width // 8
    packed = table[...]
    got = incoming[...].T
    face = got[88:89, :].astype(jnp.int32)
    groups = faces.shape[1] // LO
    listing = jnp.concatenate([faces[:, g * LO : (g + 1) * LO] for g in range(groups)], axis=0)
    f_first = (listing >> 7).astype(F32).astype(BF16)
    f_second = (listing & 127).astype(F32).astype(BF16)
    hot = one_hot_lo(face)
    f_table = jnp.concatenate([f_first, f_second], axis=0)
    picked = jnp.dot(f_table, hot, preferred_element_type=F32)
    both = picked[: 8 * groups] * 128.0 + picked[8 * groups :]
    face_hi = face >> 8
    nodes = jnp.zeros((8, width), F32)
    for g in range(groups):
        nodes = nodes + jnp.where(face_hi == g, both[8 * g : 8 * (g + 1)], 0.0)
    nodes = nodes.astype(jnp.int32)
    nodes_out[...] = nodes
    vals = [gather(packed, nodes[j : j + 1, :], own) for j in range(8)]
    matrix = [got[24 + 8 * i : 32 + 8 * i, :] for i in range(8)]
    mults = []
    for c in range(3):
        master = jnp.concatenate([vals[j][c] for j in range(8)], axis=0)
        force = jnp.zeros((8, width), F32)
        for i in range(8):
            gap = got[8 * c + i : 8 * c + i + 1, :] - jnp.sum(
                matrix[i] * master, axis=0, keepdims=True
            )
            mult = penalty * gap
            mults.append(mult)
            force = force - matrix[i] * mult
        force_out[8 * c : 8 * c + 8, :] = force
    back = jnp.concatenate(mults + [jnp.zeros((8, width), F32)], axis=0).T
    back = back.reshape(n_dom, 8, 32)
    for k in range(8):
        mult_out[:, 0, 32 * k : 32 * (k + 1)] = back[:, k, :]


def master_scatter_kernel(force, nodes, out):
    own = out.shape[0] // 3
    total = jnp.zeros(out.shape, F32)
    for j in range(8):
        values = [force[8 * c + j : 8 * c + j + 1, :] for c in range(3)]
        total = total + scatter(values, nodes[j : j + 1, :], own)
    out[...] = total


def slave_kernel(returned, slot, dual, slave, owned, master, near, far, out):
    lower, upper = by_side(near[...], far[...])
    own = owned.shape[0] // 3
    ghost = near.shape[0] // 3
    segs = slot.shape[1]
    n_dom = returned.shape[0]
    mult_rows = returned[...].reshape(n_dom, 256).T
    m1 = mult_rows.astype(BF16)
    rest = mult_rows - m1.astype(F32)
    m2 = rest.astype(BF16)
    hot = jnp.where(
        lax.broadcasted_iota(jnp.int32, (n_dom, segs), 0) == (slot[...] >> 3), 1.0, 0.0
    ).astype(BF16)
    picked = jnp.dot(
        jnp.concatenate([m1, m2], axis=1),
        jnp.concatenate([hot, hot], axis=0),
        preferred_element_type=F32,
    )
    rank = slot[...] & 7
    mult = jnp.zeros((32, segs), F32)
    for k in range(8):
        mult = mult + jnp.where(rank == k, picked[32 * k : 32 * (k + 1)], 0.0)
    total = owned[...] + master[...]
    for i in range(8):
        values = [dual[i : i + 1, :] * mult[8 * c + i : 8 * c + i + 1, :] for c in range(3)]
        total = total + scatter(values, slave[i : i + 1, :], own)
    quarters = out.shape[0]
    per = own // quarters
    for c in range(3):
        block = total[c * own : (c + 1) * own]
        for q in range(quarters):
            part = block[q * per : (q + 1) * per]
            if q == 0:
                part = jnp.concatenate(
                    [part[:ghost] + lower[c * ghost : (c + 1) * ghost], part[ghost:]], axis=0
                )
            if q == quarters - 1:
                part = jnp.concatenate(
                    [part[:-ghost], part[-ghost:] + upper[c * ghost : (c + 1) * ghost]], axis=0
                )
            out[q, c * per : (c + 1) * per, :] = part


def finish_kernel(own_part, a, b, d, out):
    per = own_part.shape[0] // 3
    total = own_part[...] + a[...] + b[...] + d[...]
    for c in range(3):
        for h in range(per):
            out[c : c + 1, h * LO : (h + 1) * LO] = total[c * per + h : c * per + h + 1, :]


def call(kernel, outs, *args, scratch=(), smem=(), hbm=(), flops=10**8):
    specs = [
        pl.BlockSpec(
            memory_space=pltpu.SMEM if i in smem else pltpu.HBM if i in hbm else pltpu.VMEM
        )
        for i in range(len(args))
    ]
    moved = sum(a.size * 4 for a in args)
    many = isinstance(outs, list)
    return pl.pallas_call(
        kernel,
        out_shape=outs,
        in_specs=specs,
        out_specs=[pl.BlockSpec(memory_space=pltpu.VMEM)] * len(outs)
        if many
        else pl.BlockSpec(memory_space=pltpu.VMEM),
        scratch_shapes=list(scratch),
        cost_estimate=pl.CostEstimate(flops=flops, transcendentals=0, bytes_accessed=moved),
        compiler_params=pltpu.CompilerParams(vmem_limit_bytes=48 * 1024 * 1024),
    )(*[pltpu.with_memory_space_constraint(a, pltpu.HBM) if i in hbm else a for i, a in enumerate(args)])


def shape(*dims):
    return jax.ShapeDtypeStruct(dims, F32)


def elements(table, near, far, connect, shear, bulk, k_shear, k_bulk):
    rows = table.shape[0] + near.shape[0] + far.shape[0]
    elems = connect.shape[1]
    return call(
        element_kernel,
        [shape(table.shape[0], LO), shape(*near.shape), shape(*far.shape)],
        table,
        near,
        far,
        connect,
        shear,
        bulk,
        k_shear,
        k_bulk,
        scratch=[
            pltpu.VMEM((rows, 2 * LO), BF16),
            pltpu.VMEM((64, elems), F32),
            pltpu.VMEM((64, 64), F32),
            pltpu.VMEM((20, LO, elems), BF16),
            pltpu.VMEM((rows, LO), F32),
        ],
        flops=ELEMENT_FLOPS,
    )


def pack(displacement, seg_slave, dual, mortar, seg_face, seg_part, seg_count, n_dom):
    own = displacement.shape[1] // LO
    segs = seg_face.shape[0]
    return call(
        pack_kernel,
        [
            shape(n_dom * 8, 128),
            jax.ShapeDtypeStruct((1, segs), jnp.int32),
            jax.ShapeDtypeStruct((3 * own, 2 * LO), BF16),
            shape(3 * GHOST // LO, LO),
            shape(3 * GHOST // LO, LO),
        ],
        displacement,
        seg_slave,
        dual,
        mortar,
        seg_face[None],
        seg_part.reshape(1, segs),
        seg_count.reshape(1, 1),
        smem=(6,),
        hbm=(0, 1, 2, 3, 4, 5),
        scratch=[
            pltpu.VMEM((3 * own, LO), F32),
            pltpu.VMEM(displacement.shape, F32),
            pltpu.VMEM(seg_slave.shape, jnp.int32),
            pltpu.VMEM(dual.shape, F32),
            pltpu.VMEM(mortar.shape, F32),
            pltpu.VMEM((1, segs), jnp.int32),
            pltpu.VMEM((1, segs), jnp.int32),
            pltpu.SemaphoreType.DMA((6,)),
        ],
    )


def master(incoming, table, face_nodes):
    width = incoming.shape[0]
    return call(
        master_kernel,
        [
            shape(width // 8, 1, 256),
            shape(24, width),
            jax.ShapeDtypeStruct((8, width), jnp.int32),
        ],
        incoming,
        table,
        face_nodes,
    )


def slave_side(returned, slot, dual, seg_slave, owned, master_part, near, far, n_sub):
    own = owned.shape[0] // 3
    return call(
        slave_kernel,
        shape(n_sub, 3 * own // n_sub, LO),
        returned,
        slot,
        dual,
        seg_slave,
        owned,
        master_part,
        near,
        far,
    )


def on_device(
    displacement,
    connect,
    shear,
    bulk,
    stiff_shear,
    stiff_bulk,
    seg_slave,
    seg_part,
    seg_face,
    face_nodes,
    dual,
    mortar,
    seg_count,
):
    nodes = displacement.shape[1]
    n_dom, n_sub = lax.axis_size("dom"), lax.axis_size("sub")
    group = sorted(range(n_dom), key=lambda part: place_in_group(part, n_dom))
    near_pairs = [(i, i ^ 1) for i in range(n_dom)]
    far_pairs = [(i, min(max(((i + 1) ^ 1) - 1, 0), n_dom - 1)) for i in range(n_dom)]
    outgoing, slot, table, near, far = pack(
        displacement, seg_slave, dual, mortar, seg_face, seg_part, seg_count, n_dom
    )
    incoming = lax.all_to_all(
        outgoing.reshape(n_dom, 8, 128), "dom", 0, 0, axis_index_groups=[group], tiled=True
    )
    near = lax.ppermute(near, "dom", near_pairs)
    far = lax.ppermute(far, "dom", far_pairs)
    owned, near, far = elements(
        table, near, far, connect, shear, bulk, stiff_shear, stiff_bulk
    )
    incoming, owned = lax.optimization_barrier((incoming, owned))
    mult, master_force, master_nodes = master(
        incoming.reshape(n_dom * 8, 128), table, face_nodes
    )
    returned = lax.all_to_all(mult, "dom", 0, 0, axis_index_groups=[group], tiled=True)
    near = lax.ppermute(near, "dom", near_pairs)
    far = lax.ppermute(far, "dom", far_pairs)
    master_part = call(
        master_scatter_kernel, shape(3 * nodes // LO, LO), master_force, master_nodes
    )
    blocks = slave_side(
        returned, slot, dual, seg_slave, owned, master_part, near, far, n_sub
    )
    me = lax.axis_index("sub")
    sent = [
        lax.ppermute(
            lax.dynamic_index_in_dim(blocks, (me + k) % n_sub, 0, keepdims=False),
            "sub",
            [(s, (s + k) % n_sub) for s in range(n_sub)],
        )
        for k in range(1, n_sub)
    ]
    mine = lax.dynamic_index_in_dim(blocks, me, 0, keepdims=False)
    return call(finish_kernel, shape(3, nodes // n_sub), mine, *sent)


def solution(mesh):
    placed = (
        P(None, "dom"),
        P(None, ("dom", "sub")),
        P(("dom", "sub")),
        P(("dom", "sub")),
        P(),
        P(),
        P(None, ("dom", "sub")),
        P(("dom", "sub"), None),
        P(("dom", "sub")),
        P(None, "dom"),
        P(None, ("dom", "sub")),
        P(None, ("dom", "sub")),
        P(("dom", "sub")),
    )
    return jax.shard_map(
        on_device, mesh=mesh, in_specs=placed, out_specs=P(None, ("dom", "sub")), check_vma=False
    )
```
